512 devices in a mesh: dp: 32 (over z, core), shard: 16 (over y, x).
Axes of the slice: x: 4, y: 4, z: 16, core: 2. Of those that a mesh axis runs over, the one named last changes fastest.
Arguments:
- points: bfloat16 [131072, 1024], P(('dp', 'shard'))
- first_center: bfloat16 [1024], replicated, may hold values from -0.1875 to 0.1875
- counts: int32 [3, 32, 16], P(None, 'dp', 'shard'), may hold values from 0 to 4, as said below
- cand_index: int32 [3, 32, 16, 4], P(None, 'dp', 'shard'), may hold values from 0 to 255, as said below
Outputs:
- min_dist: float32 [131072], P(('dp', 'shard'))
- weights: float32 [131072], P(('dp', 'shard'))
- potentials: float32 [4], replicated
The draws below stay inside these ranges and needn't reach their ends.
Inputs may be any that keep to these rules, and one draw needn't show every extreme that they name: In each round the counts of the 16 devices of one dp index sum to 16, so a round has 512 candidates; in each round and dp index some device has exactly 4. `cand_index`: each device's list in a round holds distinct local row numbers; only its first counts entries are candidates.
All inputs are finite; a program needn't handle non-finite values.
Results may differ from the reference program's by a relative error of at most 0.0003.
Values may be sent and summed in bfloat16 or wider, within the bound.
No kernel may reach another device: no remote copies, remote signals or barrier semaphores. Data moves between devices by JAX's collectives and lax.ppermute only.
A program may use at most 64 MiB of HBM per device.

```python
import jax
import jax.numpy as jnp
from jax import lax

D = 1024
ROWS_DEV = 256
CANDS = 512
ROUNDS = 3
GROUPS = 32
GROUP_SIZE = 16
CAP = 4
GROUP_CANDS = 16
ROWS = 131072
DEVICES = 512


cluster_count = 256


def draw_points(key, part):
    keys = jax.random.split(key, 4)
    means = jax.random.normal(keys[0], (cluster_count, D), jnp.float32) / jnp.sqrt(float(D))
    member = jax.random.randint(keys[1], (ROWS,), 0, cluster_count)
    base = jnp.take(means, member, axis=0)
    trend = jnp.sqrt(1.0 + 2.0 * jnp.arange(ROWS, dtype=jnp.float32) / ROWS)[:, None]
    noise = 0.5 * jax.random.normal(keys[2], (ROWS, D), jnp.float32) / jnp.sqrt(float(D))
    spread = jnp.exp(jax.random.uniform(keys[3], (ROWS, 1), jnp.float32) * jnp.log(3.2))
    values = spread * trend * (base + noise)
    return values.astype(jnp.bfloat16)


def group_counts(key):
    key_hot, key_slots = jax.random.split(key)
    hot = jax.random.randint(key_hot, (), 0, GROUP_SIZE)
    slot_total = (GROUP_SIZE - 1) * CAP
    order = jax.random.permutation(key_slots, slot_total)
    taken = (jnp.arange(slot_total) < GROUP_CANDS - CAP).astype(jnp.int32)
    owner = order // CAP
    others = jnp.sum((owner[:, None] == jnp.arange(GROUP_SIZE - 1)[None, :]).astype(jnp.int32) * taken[:, None], axis=0)
    device = jnp.arange(GROUP_SIZE)
    other_pos = jnp.clip(device - (device > hot).astype(jnp.int32), 0, GROUP_SIZE - 2)
    return jnp.where(device == hot, CAP, jnp.take(others, other_pos)).astype(jnp.int32)


def draw_counts(key, part):
    keys = jax.random.split(jax.random.fold_in(key, 11), ROUNDS * GROUPS)
    values = jax.vmap(group_counts)(keys)
    return values.reshape(ROUNDS, GROUPS, GROUP_SIZE).astype(jnp.int32)


def draw_cand_index(key, part):
    keys = jax.random.split(jax.random.fold_in(key, 23), ROUNDS * GROUPS * GROUP_SIZE)
    values = jax.vmap(lambda k: jax.random.permutation(k, ROWS_DEV)[:CAP])(keys)
    return values.reshape(ROUNDS, GROUPS, GROUP_SIZE, CAP).astype(jnp.int32)


def scatter_about(stream_key, dims, scale, bound, held_as=jnp.bfloat16):
    return jnp.clip(scale * jax.random.normal(stream_key, dims, jnp.float32), -bound, bound).astype(held_as)


def setup_inputs(seed: int = 0) -> dict:
    streams_of = jax.random.split(jax.random.key(seed), 5)
    return {
        "points": draw_points(jax.random.fold_in(streams_of[4], 71), 0),
        "first_center": scatter_about(streams_of[1], (D,), D ** -0.5, 0.1875),
        "counts": draw_counts(jax.random.fold_in(streams_of[4], 71), 0),
        "cand_index": draw_cand_index(jax.random.fold_in(streams_of[4], 71), 0),
    }


def pair_dist(rows, cands):
    prod = jnp.dot(rows, cands.T, preferred_element_type=jnp.float32)
    rows_norm = jnp.sum(jnp.square(rows.astype(jnp.float32)), axis=1)
    cand_norm = jnp.sum(jnp.square(cands.astype(jnp.float32)), axis=1)
    return jnp.maximum(rows_norm[:, None] + cand_norm[None, :] - 2.0 * prod, 0.0)


def block_min(points, cands):
    block_rows = ROWS_DEV * 8
    blocks = points.reshape(ROWS // block_rows, block_rows, D)
    least = lax.map(lambda blk: jnp.min(pair_dist(blk, cands), axis=1), blocks)
    return least.reshape(ROWS)


def reference(points, first_center, counts, cand_index):
    running = block_min(points, first_center[None, :])
    sums = [jnp.sum(running)]
    for step in range(ROUNDS):
        each_count = counts[step].reshape(DEVICES)
        local_rows = cand_index[step].reshape(DEVICES, CAP)
        global_rows = jnp.arange(DEVICES, dtype=jnp.int32)[:, None] * ROWS_DEV + local_rows
        valid = jnp.arange(CAP, dtype=jnp.int32)[None, :] < each_count[:, None]
        chosen = jnp.nonzero(valid.reshape(-1), size=CANDS)[0].astype(jnp.int32)
        rows = jnp.take(global_rows.reshape(-1), chosen)
        cands = jnp.take(points, rows, axis=0)
        running = jnp.minimum(running, block_min(points, cands))
        sums.append(jnp.sum(running))
    potentials = jnp.stack(sums)
    weights = running * (ROWS / potentials[-1])
    return running, weights, potentials
```

```python
import jax
import jax.numpy as jnp
from jax import lax
from jax.experimental import pallas as pl
from jax.experimental.pallas import tpu as pltpu
from jax.sharding import Mesh
from jax.sharding import PartitionSpec as P

D = 1024
ROWS_DEV = 256
ROUNDS = 3
CAP = 4
ROWS = 131072
NZ, NC, NY, NX = 16, 2, 4, 4
PLANE = NY * NX
BLK = 16
CNT_ROW = ROUNDS * CAP
KEEP = ROUNDS * NZ
HALF = KEEP * PLANE

VMEM = pltpu.VMEM
SMEM = pltpu.SMEM
F32 = jnp.float32
BF16 = jnp.bfloat16


def iota(shape, dim):
    return lax.broadcasted_iota(jnp.int32, shape, dim)


def one_hot(cond):
    return jnp.where(cond, 1.0, 0.0).astype(BF16)


def dot_nt(a, b):
    return lax.dot_general(a, b, (((1,), (1,)), ((), ())), preferred_element_type=F32)


def pack_kernel(cnt_ref, idx_ref, pts_ref, out_ref):
    sub = iota((BLK, ROWS_DEV), 0)
    lane = iota((BLK, ROWS_DEV), 1)
    want = jnp.full((BLK, ROWS_DEV), -1, jnp.int32)
    for q in range(CNT_ROW):
        want = jnp.where(sub == q, idx_ref[q], want)
    rows = jnp.dot(one_hot(lane == want), pts_ref[...], preferred_element_type=F32)
    sub = iota((BLK, D), 0)
    lane = iota((BLK, D), 1)
    for r in range(ROUNDS):
        here = jnp.logical_and(sub == CNT_ROW, lane == r)
        rows = jnp.where(here, cnt_ref[r].astype(F32), rows)
    rows = rows.astype(BF16)
    for i in range(PLANE):
        out_ref[i] = rows


def compact_kernel(recv_ref, out_ref):
    place = lax.axis_index("y") * NX + lax.axis_index("x")
    n = PLANE * BLK
    head = recv_ref[:, 0:128]
    src = iota((n, n), 0)
    dst = iota((n, n), 1)
    is_cnt = src % BLK == CNT_ROW
    own = one_hot(jnp.logical_and(is_cnt, src // BLK == dst // BLK))
    before = one_hot(jnp.logical_and(is_cnt, src // BLK < dst // BLK))
    contract = (((0,), (0,)), ((), ()))
    cnt = lax.dot_general(head, own, contract, preferred_element_type=F32)[:16]
    off = lax.dot_general(head, before, contract, preferred_element_type=F32)[:16]
    r = iota((16, n), 0)
    q = iota((16, n), 1) % BLK
    j = (q % CAP).astype(F32)
    live = jnp.logical_and(q < CNT_ROW, q // CAP == r)
    live = jnp.logical_and(live, j < cnt)
    live = jnp.logical_and(live, off + j == place.astype(F32))
    rows = jnp.dot(one_hot(live), recv_ref[...], preferred_element_type=F32)
    rows = rows[0:4].astype(BF16)
    for i in range(NZ):
        out_ref[i] = rows


def spread_kernel(recv_ref, out_ref, tmp_ref):
    for z in range(NZ):
        tmp_ref[4 * z : 4 * z + 4, :] = recv_ref[z].astype(F32)
    m = iota((KEEP, 4 * NZ), 0)
    k = iota((KEEP, 4 * NZ), 1)
    sel = one_hot(k == 4 * (m % NZ) + m // NZ)
    rows = jnp.dot(sel, tmp_ref[...].astype(BF16), preferred_element_type=F32)
    rows = rows.astype(BF16)
    for i in range(PLANE):
        out_ref[i] = rows


def round_mins(cands_ref, pts):
    cands = cands_ref[...]
    prod = dot_nt(cands, pts)
    wide = cands.astype(F32)
    norm = jnp.sum(wide * wide, axis=1, keepdims=True)
    val = (norm - 2.0 * prod).reshape(PLANE, ROUNDS, NZ, ROWS_DEV)
    least = jnp.min(jnp.min(val, axis=0), axis=1)
    return [least[r : r + 1] for r in range(ROUNDS)]


def own_kernel(pts_ref, center_ref, cands_ref, out_ref):
    pts = pts_ref[...]
    wide = pts.astype(F32)
    sq = wide * wide
    hi = sq.astype(BF16)
    lo = (sq - hi.astype(F32)).astype(BF16)
    ones = jnp.ones((16, D), BF16)
    rows_norm = (dot_nt(ones, hi) + dot_nt(ones, lo))[0:1]
    center = jnp.broadcast_to(center_ref[...], (16, D))
    cwide = center.astype(F32)
    cnorm = jnp.sum(cwide * cwide, axis=1, keepdims=True)
    first = (cnorm - 2.0 * dot_nt(center, pts))[0:1]
    mins = round_mins(cands_ref, pts)
    out_ref[0:1] = rows_norm
    out_ref[1:2] = first
    for r in range(ROUNDS):
        out_ref[2 + r : 3 + r] = mins[r]


def other_kernel(pts_ref, own_ref, cands_ref, run_ref, sums_ref):
    mins = round_mins(cands_ref, pts_ref[...])
    rows_norm = own_ref[0:1]
    running = jnp.maximum(rows_norm + own_ref[1:2], 0.0)
    lane = iota((PLANE, 128), 1)
    sums = jnp.where(lane == 0, jnp.sum(running), 0.0)
    for r in range(ROUNDS):
        least = jnp.minimum(own_ref[2 + r : 3 + r], mins[r])
        running = jnp.minimum(running, jnp.maximum(rows_norm + least, 0.0))
        sums = jnp.where(lane == r + 1, jnp.sum(running), sums)
    run_ref[...] = running
    sums_ref[...] = sums


def relay_kernel(recv_ref, out_ref):
    total = jnp.sum(recv_ref[...], axis=0, keepdims=True)
    out_ref[...] = jnp.broadcast_to(total, (NZ * NC, 128))


def final_kernel(recv_ref, run_ref, dist_ref, weight_ref, pot_ref):
    total = jnp.sum(recv_ref[...], axis=0, keepdims=True)
    lane = iota((1, 128), 1)
    last = jnp.sum(jnp.where(lane == ROUNDS, total, 0.0), axis=1, keepdims=True)
    running = run_ref[...]
    dist_ref[...] = running.reshape(ROWS_DEV)
    weight_ref[...] = (running * (ROWS / last)).reshape(ROWS_DEV)
    pot_ref[...] = total.reshape(128)[0 : ROUNDS + 1]


def vspec():
    return pl.BlockSpec(memory_space=VMEM)


def sspec():
    return pl.BlockSpec(memory_space=SMEM)


def call(kernel, ins, outs, scratch=(), name=None):
    shapes = [jax.ShapeDtypeStruct(s, d) for s, d in outs]
    single = len(shapes) == 1
    return pl.pallas_call(
        kernel,
        in_specs=ins,
        out_specs=vspec() if single else [vspec() for _ in shapes],
        out_shape=shapes[0] if single else shapes,
        scratch_shapes=list(scratch),
        name=name,
    )


def body(points, first_center, counts, cand_index):
    pack = call(pack_kernel, [sspec(), sspec(), vspec()], [((PLANE, BLK, D), BF16)], name="pack")
    blocks = pack(counts.reshape(ROUNDS), cand_index.reshape(ROUNDS * CAP), points)
    blocks = lax.all_to_all(blocks, ("y", "x"), 0, 0)
    compact = call(compact_kernel, [vspec()], [((NZ, 4, D), BF16)], name="compact")
    mine = compact(blocks.reshape(PLANE * BLK, D))
    mine = lax.all_to_all(mine, "z", 0, 0)
    spread = call(spread_kernel, [vspec()], [((PLANE, KEEP, D), BF16)], [VMEM((4 * NZ, D), F32)], name="spread")
    cands = lax.all_to_all(spread(mine), ("y", "x"), 0, 0).reshape(HALF, D)
    others = lax.ppermute(cands, "c", [(0, 1), (1, 0)])
    own = call(own_kernel, [vspec()] * 3, [((8, ROWS_DEV), F32)], name="own")
    found = own(points, first_center.reshape(1, D), cands)
    other = call(other_kernel, [vspec()] * 3, [((1, ROWS_DEV), F32), ((PLANE, 128), F32)], name="other")
    running, sums = other(points, found, others)
    sums = lax.all_to_all(sums, ("y", "x"), 0, 0)
    relay = call(relay_kernel, [vspec()], [((NZ * NC, 128), F32)], name="relay")
    sums = lax.all_to_all(relay(sums), ("z", "c"), 0, 0)
    final = call(
        final_kernel,
        [vspec()] * 2,
        [((ROWS_DEV,), F32), ((ROWS_DEV,), F32), ((ROUNDS + 1,), F32)],
        name="final",
    )
    return tuple(final(sums, running))


def solution(mesh):
    axes = ("z", "c", "y", "x")
    grid = Mesh(mesh.devices.reshape(NZ, NC, NY, NX), axes)
    placed = (P(axes, None), P(), P(None, ("z", "c"), ("y", "x")), P(None, ("z", "c"), ("y", "x"), None))
    return jax.shard_map(
        body,
        mesh=grid,
        in_specs=placed,
        out_specs=(P(axes), P(axes), P()),
        check_vma=False,
    )
```

```python
import jax
import jax.numpy as jnp
from jax import lax
from jax.experimental import pallas as pl
from jax.experimental.pallas import tpu as pltpu
from jax.sharding import Mesh
from jax.sharding import PartitionSpec as P

D = 1024
ROWS_DEV = 256
ROUNDS = 3
CAP = 4
ROWS = 131072
NZ, NC, NY, NX = 16, 2, 4, 4
PLANE = NY * NX
BLK = 16
CNT_ROW = ROUNDS * CAP
KEEP = ROUNDS * NZ
HALF = KEEP * PLANE

VMEM = pltpu.VMEM
SMEM = pltpu.SMEM
F32 = jnp.float32
BF16 = jnp.bfloat16


def iota(shape, dim):
    return lax.broadcasted_iota(jnp.int32, shape, dim)


def one_hot(cond):
    return jnp.where(cond, 1.0, 0.0).astype(BF16)


def dot_nt(a, b):
    return lax.dot_general(a, b, (((1,), (1,)), ((), ())), preferred_element_type=F32)


def pack_kernel(cnt_hbm, idx_hbm, pts_hbm, out_ref, cnt_ref, idx_ref, pts_ref, sem):
    fetch_idx = pltpu.make_async_copy(idx_hbm, idx_ref, sem.at[0])
    fetch_cnt = pltpu.make_async_copy(cnt_hbm, cnt_ref, sem.at[1])
    fetch = pltpu.make_async_copy(pts_hbm, pts_ref, sem.at[2])
    fetch_idx.start()
    fetch_cnt.start()
    fetch.start()
    fetch_idx.wait()
    fetch_cnt.wait()
    sub = iota((BLK, ROWS_DEV), 0)
    lane = iota((BLK, ROWS_DEV), 1)
    want = jnp.full((BLK, ROWS_DEV), -1, jnp.int32)
    for q in range(CNT_ROW):
        want = jnp.where(sub == q, idx_ref[q // CAP, 0, 0, q % CAP], want)
    fetch.wait()
    rows = jnp.dot(one_hot(lane == want), pts_ref[...], preferred_element_type=F32)
    sub = iota((BLK, D), 0)
    lane = iota((BLK, D), 1)
    for r in range(ROUNDS):
        here = jnp.logical_and(sub == CNT_ROW, lane == r)
        rows = jnp.where(here, cnt_ref[r].astype(F32), rows)
    rows = rows.astype(BF16)
    for i in range(PLANE):
        out_ref[i] = rows


def compact_kernel(recv_ref, out_ref):
    place = lax.axis_index("y") * NX + lax.axis_index("x")
    n = PLANE * BLK
    head = recv_ref[:, 0:128]
    src = iota((n, n), 0)
    dst = iota((n, n), 1)
    is_cnt = src % BLK == CNT_ROW
    own = one_hot(jnp.logical_and(is_cnt, src // BLK == dst // BLK))
    before = one_hot(jnp.logical_and(is_cnt, src // BLK < dst // BLK))
    contract = (((0,), (0,)), ((), ()))
    cnt = lax.dot_general(head, own, contract, preferred_element_type=F32)[:16]
    off = lax.dot_general(head, before, contract, preferred_element_type=F32)[:16]
    r = iota((16, n), 0)
    q = iota((16, n), 1) % BLK
    j = (q % CAP).astype(F32)
    live = jnp.logical_and(q < CNT_ROW, q // CAP == r)
    live = jnp.logical_and(live, j < cnt)
    live = jnp.logical_and(live, off + j == place.astype(F32))
    rows = jnp.dot(one_hot(live), recv_ref[...], preferred_element_type=F32)
    rows = rows[0:4].astype(BF16)
    for i in range(NZ):
        out_ref[i] = rows


def spread_kernel(recv_ref, out_ref, tmp_ref):
    for z in range(NZ):
        tmp_ref[4 * z : 4 * z + 4, :] = recv_ref[z].astype(F32)
    m = iota((KEEP, 4 * NZ), 0)
    k = iota((KEEP, 4 * NZ), 1)
    sel = one_hot(k == 4 * (m % NZ) + m // NZ)
    rows = jnp.dot(sel, tmp_ref[...].astype(BF16), preferred_element_type=F32)
    rows = rows.astype(BF16)
    for i in range(PLANE):
        out_ref[i] = rows


def round_mins(cands_ref, pts):
    cands = cands_ref[...]
    prod = dot_nt(cands, pts)
    wide = cands.astype(F32)
    norm = jnp.sum(wide * wide, axis=1, keepdims=True)
    val = (norm - 2.0 * prod).reshape(PLANE, ROUNDS, NZ, ROWS_DEV)
    least = jnp.min(jnp.min(val, axis=0), axis=1)
    return [least[r : r + 1] for r in range(ROUNDS)]


def own_kernel(pts_ref, center_ref, cands_ref, out_ref):
    pts = pts_ref[...]
    wide = pts.astype(F32)
    sq = wide * wide
    hi = sq.astype(BF16)
    lo = (sq - hi.astype(F32)).astype(BF16)
    ones = jnp.ones((16, D), BF16)
    rows_norm = (dot_nt(ones, hi) + dot_nt(ones, lo))[0:1]
    center = jnp.broadcast_to(center_ref[...].reshape(1, D), (16, D))
    cwide = center.astype(F32)
    cnorm = jnp.sum(cwide * cwide, axis=1, keepdims=True)
    first = (cnorm - 2.0 * dot_nt(center, pts))[0:1]
    mins = round_mins(cands_ref, pts)
    out_ref[0:1] = rows_norm
    out_ref[1:2] = first
    for r in range(ROUNDS):
        out_ref[2 + r : 3 + r] = mins[r]


def other_kernel(pts_ref, own_ref, cands_ref, run_ref, sums_ref):
    mins = round_mins(cands_ref, pts_ref[...])
    rows_norm = own_ref[0:1]
    running = jnp.maximum(rows_norm + own_ref[1:2], 0.0)
    lane = iota((PLANE, 128), 1)
    sums = jnp.where(lane == 0, jnp.sum(running), 0.0)
    for r in range(ROUNDS):
        least = jnp.minimum(own_ref[2 + r : 3 + r], mins[r])
        running = jnp.minimum(running, jnp.maximum(rows_norm + least, 0.0))
        sums = jnp.where(lane == r + 1, jnp.sum(running), sums)
    run_ref[...] = running
    sums_ref[...] = sums


def relay_kernel(recv_ref, out_ref):
    total = jnp.sum(recv_ref[...], axis=0, keepdims=True)
    out_ref[...] = jnp.broadcast_to(total, (NZ * NC, 128))


def final_kernel(recv_ref, run_ref, dist_ref, weight_ref, pot_ref):
    total = jnp.sum(recv_ref[...], axis=0, keepdims=True)
    lane = iota((1, 128), 1)
    last = jnp.sum(jnp.where(lane == ROUNDS, total, 0.0), axis=1, keepdims=True)
    running = run_ref[...]
    dist_ref[...] = running.reshape(ROWS_DEV)
    weight_ref[...] = (running * (ROWS / last)).reshape(ROWS_DEV)
    pot_ref[...] = total.reshape(128)[0 : ROUNDS + 1]


def vspec():
    return pl.BlockSpec(memory_space=VMEM)


def call(kernel, ins, outs, scratch=(), name=None, near=True):
    shapes = [VMEM(s, d) if near else jax.ShapeDtypeStruct(s, d) for s, d in outs]
    single = len(shapes) == 1
    kern = pl.pallas_call(
        kernel,
        in_specs=ins,
        out_specs=vspec() if single else [vspec() for _ in shapes],
        out_shape=shapes[0] if single else shapes,
        scratch_shapes=list(scratch),
        compiler_params=pltpu.CompilerParams(vmem_limit_bytes=16 << 20),
        name=name,
    )

    def run(*args):
        placed = []
        for a, i in zip(args, ins):
            space = VMEM if i.memory_space == VMEM else pltpu.HBM
            placed.append(pltpu.with_memory_space_constraint(a, space))
        return kern(*placed)

    return run


def body(points, first_center, counts, cand_index):
    pack = call(
        pack_kernel,
        [pl.BlockSpec(memory_space=pl.ANY)] * 3,
        [((PLANE, BLK, D), BF16)],
        [
            SMEM((ROUNDS,), jnp.int32),
            SMEM((ROUNDS, 1, 1, CAP), jnp.int32),
            VMEM((ROWS_DEV, D), BF16),
            pltpu.SemaphoreType.DMA((3,)),
        ],
        name="pack",
    )
    blocks = pack(counts.reshape(ROUNDS), cand_index, points)
    blocks = lax.all_to_all(blocks, ("y", "x"), 0, 0)
    compact = call(compact_kernel, [vspec()], [((NZ, 4, D), BF16)], name="compact")
    mine = compact(blocks.reshape(PLANE * BLK, D))
    mine = lax.all_to_all(mine, "z", 0, 0)
    spread = call(spread_kernel, [vspec()], [((PLANE, KEEP, D), BF16)], [VMEM((4 * NZ, D), F32)], name="spread")
    cands = lax.all_to_all(spread(mine), ("y", "x"), 0, 0).reshape(HALF, D)
    others = lax.ppermute(cands, "c", [(0, 1), (1, 0)])
    own = call(own_kernel, [vspec()] * 3, [((8, ROWS_DEV), F32)], name="own")
    found = own(points, first_center, cands)
    other = call(other_kernel, [vspec()] * 3, [((1, ROWS_DEV), F32), ((PLANE, 128), F32)], name="other")
    running, sums = other(points, found, others)
    sums = lax.all_to_all(sums, ("y", "x"), 0, 0)
    relay = call(relay_kernel, [vspec()], [((NZ * NC, 128), F32)], name="relay")
    sums = lax.all_to_all(relay(sums), ("z", "c"), 0, 0)
    final = call(
        final_kernel,
        [vspec()] * 2,
        [((ROWS_DEV,), F32), ((ROWS_DEV,), F32), ((ROUNDS + 1,), F32)],
        name="final",
        near=False,
    )
    return tuple(final(sums, running))


def solution(mesh):
    axes = ("z", "c", "y", "x")
    grid = Mesh(mesh.devices.reshape(NZ, NC, NY, NX), axes)
    placed = (P(axes, None), P(), P(None, ("z", "c"), ("y", "x")), P(None, ("z", "c"), ("y", "x"), None))
    return jax.shard_map(
        body,
        mesh=grid,
        in_specs=placed,
        out_specs=(P(axes), P(axes), P()),
        check_vma=False,
    )
```

```python
import jax
import jax.numpy as jnp
from jax import lax
from jax.experimental import pallas as pl
from jax.experimental.pallas import tpu as pltpu
from jax.sharding import Mesh
from jax.sharding import PartitionSpec as P

D = 1024
ROWS_DEV = 256
ROUNDS = 3
CAP = 4
ROWS = 131072
NZ, NC, NY, NX = 16, 2, 4, 4
PLANE = NY * NX
BLK = 16
CNT_ROW = ROUNDS * CAP
CLASSES = 4
PER = PLANE // CLASSES
PIECE = ROUNDS * NZ * PER

VMEM = pltpu.VMEM
SMEM = pltpu.SMEM
F32 = jnp.float32
BF16 = jnp.bfloat16


def iota(shape, dim):
    return lax.broadcasted_iota(jnp.int32, shape, dim)


def one_hot(cond):
    return jnp.where(cond, 1.0, 0.0).astype(BF16)


def dot_nt(a, b):
    return lax.dot_general(a, b, (((1,), (1,)), ((), ())), preferred_element_type=F32)


def pack_kernel(cnt_hbm, idx_hbm, pts_hbm, out_ref, cnt_ref, idx_ref, pts_ref, sem):
    fetch_idx = pltpu.make_async_copy(idx_hbm, idx_ref, sem.at[0])
    fetch_cnt = pltpu.make_async_copy(cnt_hbm, cnt_ref, sem.at[1])
    fetch = pltpu.make_async_copy(pts_hbm, pts_ref, sem.at[2])
    fetch_idx.start()
    fetch_cnt.start()
    fetch.start()
    fetch_idx.wait()
    fetch_cnt.wait()
    sub = iota((BLK, ROWS_DEV), 0)
    lane = iota((BLK, ROWS_DEV), 1)
    want = jnp.full((BLK, ROWS_DEV), -1, jnp.int32)
    for q in range(CNT_ROW):
        want = jnp.where(sub == q, idx_ref[q // CAP, 0, 0, q % CAP], want)
    fetch.wait()
    rows = jnp.dot(one_hot(lane == want), pts_ref[...], preferred_element_type=F32)
    sub = iota((BLK, D), 0)
    lane = iota((BLK, D), 1)
    for r in range(ROUNDS):
        here = jnp.logical_and(sub == CNT_ROW, lane == r)
        rows = jnp.where(here, cnt_ref[r].astype(F32), rows)
    rows = rows.astype(BF16)
    for i in range(PLANE):
        out_ref[i] = rows


def compact_kernel(recv_ref, out_ref):
    place = (lax.axis_index("x") + 2 * lax.axis_index("y")) % CLASSES
    n = PLANE * BLK
    head = recv_ref[:, 0:128]
    src = iota((n, n), 0)
    dst = iota((n, n), 1)
    is_cnt = src % BLK == CNT_ROW
    own = one_hot(jnp.logical_and(is_cnt, src // BLK == dst // BLK))
    before = one_hot(jnp.logical_and(is_cnt, src // BLK < dst // BLK))
    pick = one_hot(iota((128, 16), 0) == iota((128, 16), 1) // PER)
    head = jnp.dot(head, pick, preferred_element_type=F32).astype(BF16)
    contract = (((0,), (0,)), ((), ()))
    cnt = lax.dot_general(head, own, contract, preferred_element_type=F32)
    off = lax.dot_general(head, before, contract, preferred_element_type=F32)
    m = iota((16, n), 0)
    q = iota((16, n), 1) % BLK
    j = (q % CAP).astype(F32)
    slot = (place * PER + m % PER).astype(F32)
    live = jnp.logical_and(q < CNT_ROW, q // CAP == m // PER)
    live = jnp.logical_and(live, j < cnt)
    live = jnp.logical_and(live, off + j == slot)
    rows = jnp.dot(one_hot(live), recv_ref[...], preferred_element_type=F32).astype(BF16)
    for r in range(ROUNDS):
        part = rows[r * PER : (r + 1) * PER]
        for i in range(NZ):
            out_ref[i, r] = part


def join_kernel(recv_ref, out_ref, tmp_ref):
    for r in range(ROUNDS):
        for z in range(NZ):
            at = (r * NZ + z) * PER
            tmp_ref[at : at + PER, :] = recv_ref[z, r].astype(F32)
    out_ref[...] = tmp_ref[...].astype(BF16)


def piece_mins(piece_ref, pts):
    cands = piece_ref[...]
    prod = dot_nt(cands, pts)
    wide = cands.astype(F32)
    norm = jnp.sum(wide * wide, axis=1, keepdims=True)
    val = (norm - 2.0 * prod).reshape(ROUNDS, NZ * PER, ROWS_DEV)
    least = jnp.min(val, axis=1)
    return [least[r : r + 1] for r in range(ROUNDS)]


def own_kernel(pts_ref, center_ref, piece_ref, out_ref):
    pts = pts_ref[...]
    wide = pts.astype(F32)
    sq = wide * wide
    hi = sq.astype(BF16)
    lo = (sq - hi.astype(F32)).astype(BF16)
    ones = jnp.ones((16, D), BF16)
    rows_norm = (dot_nt(ones, hi) + dot_nt(ones, lo))[0:1]
    center = jnp.broadcast_to(center_ref[...].reshape(1, D), (16, D))
    cwide = center.astype(F32)
    cnorm = jnp.sum(cwide * cwide, axis=1, keepdims=True)
    first = (cnorm - 2.0 * dot_nt(center, pts))[0:1]
    mins = piece_mins(piece_ref, pts)
    out_ref[0:1] = rows_norm
    out_ref[1:2] = first
    for r in range(ROUNDS):
        out_ref[2 + r : 3 + r] = mins[r]


def fold_kernel(pts_ref, found_ref, *refs):
    *pieces, out_ref = refs
    pts = pts_ref[...]
    out_ref[0:2] = found_ref[0:2]
    least = [found_ref[2 + r : 3 + r] for r in range(ROUNDS)]
    for piece in pieces:
        least = [jnp.minimum(a, b) for a, b in zip(least, piece_mins(piece, pts))]
    for r in range(ROUNDS):
        out_ref[2 + r : 3 + r] = least[r]


def last_kernel(pts_ref, found_ref, *refs):
    *pieces, run_ref, sums_ref = refs
    pts = pts_ref[...]
    rows_norm = found_ref[0:1]
    least = [found_ref[2 + r : 3 + r] for r in range(ROUNDS)]
    for piece in pieces:
        least = [jnp.minimum(a, b) for a, b in zip(least, piece_mins(piece, pts))]
    running = jnp.maximum(rows_norm + found_ref[1:2], 0.0)
    lane = iota((PLANE, 128), 1)
    sums = jnp.where(lane == 0, jnp.sum(running), 0.0)
    for r in range(ROUNDS):
        running = jnp.minimum(running, jnp.maximum(rows_norm + least[r], 0.0))
        sums = jnp.where(lane == r + 1, jnp.sum(running), sums)
    run_ref[...] = running
    sums_ref[...] = sums


def relay_kernel(recv_ref, out_ref):
    total = jnp.sum(recv_ref[...], axis=0, keepdims=True)
    out_ref[...] = jnp.broadcast_to(total, (NZ * NC, 128))


def final_kernel(recv_ref, run_ref, dist_ref, weight_ref, pot_ref):
    total = jnp.sum(recv_ref[...], axis=0, keepdims=True)
    lane = iota((1, 128), 1)
    last = jnp.sum(jnp.where(lane == ROUNDS, total, 0.0), axis=1, keepdims=True)
    running = run_ref[...]
    dist_ref[...] = running.reshape(ROWS_DEV)
    weight_ref[...] = (running * (ROWS / last)).reshape(ROWS_DEV)
    pot_ref[...] = total.reshape(128)[0 : ROUNDS + 1]


def vspec():
    return pl.BlockSpec(memory_space=VMEM)


def call(kernel, ins, outs, scratch=(), name=None, near=True):
    shapes = [VMEM(s, d) if near else jax.ShapeDtypeStruct(s, d) for s, d in outs]
    single = len(shapes) == 1
    kern = pl.pallas_call(
        kernel,
        in_specs=ins,
        out_specs=vspec() if single else [vspec() for _ in shapes],
        out_shape=shapes[0] if single else shapes,
        scratch_shapes=list(scratch),
        compiler_params=pltpu.CompilerParams(vmem_limit_bytes=16 << 20),
        name=name,
    )

    def run(*args):
        placed = []
        for a, i in zip(args, ins):
            space = VMEM if i.memory_space == VMEM else pltpu.HBM
            placed.append(pltpu.with_memory_space_constraint(a, space))
        return kern(*placed)

    return run


def body(points, first_center, counts, cand_index):
    pack = call(
        pack_kernel,
        [pl.BlockSpec(memory_space=pl.ANY)] * 3,
        [((PLANE, BLK, D), BF16)],
        [
            SMEM((ROUNDS,), jnp.int32),
            SMEM((ROUNDS, 1, 1, CAP), jnp.int32),
            VMEM((ROWS_DEV, D), BF16),
            pltpu.SemaphoreType.DMA((3,)),
        ],
        name="pack",
    )
    blocks = pack(counts.reshape(ROUNDS), cand_index, points)
    blocks = lax.all_to_all(blocks, ("y", "x"), 0, 0)
    compact = call(compact_kernel, [vspec()], [((NZ, ROUNDS, PER, D), BF16)], name="compact")
    mine = compact(blocks.reshape(PLANE * BLK, D))
    mine = lax.all_to_all(mine, "z", 0, 0)
    join = call(join_kernel, [vspec()], [((PIECE, D), BF16)], [VMEM((PIECE, D), F32)], name="join")
    piece = join(mine)

    def swap(rows):
        return lax.ppermute(rows, "c", [(0, 1), (1, 0)])

    right = lax.ppermute(piece, "x", [((i + 1) % NX, i) for i in range(NX)])
    left = lax.ppermute(piece, "x", [(i, (i + 1) % NX) for i in range(NX)])
    down = lax.ppermute(piece, "y", [((i + 1) % NY, i) for i in range(NY)])
    own = call(own_kernel, [vspec()] * 3, [((8, ROWS_DEV), F32)], name="own")
    found = own(points, first_center, piece)
    fold = call(fold_kernel, [vspec()] * 6, [((8, ROWS_DEV), F32)], name="fold")
    found = fold(points, found, right, left, down, swap(piece))
    last = call(last_kernel, [vspec()] * 5, [((1, ROWS_DEV), F32), ((PLANE, 128), F32)], name="last")
    running, sums = last(points, found, swap(right), swap(left), swap(down))
    sums = lax.all_to_all(sums, ("y", "x"), 0, 0)
    relay = call(relay_kernel, [vspec()], [((NZ * NC, 128), F32)], name="relay")
    sums = lax.all_to_all(relay(sums), ("z", "c"), 0, 0)
    final = call(
        final_kernel,
        [vspec()] * 2,
        [((ROWS_DEV,), F32), ((ROWS_DEV,), F32), ((ROUNDS + 1,), F32)],
        name="final",
        near=False,
    )
    return tuple(final(sums, running))


def solution(mesh):
    axes = ("z", "c", "y", "x")
    grid = Mesh(mesh.devices.reshape(NZ, NC, NY, NX), axes)
    placed = (P(axes, None), P(), P(None, ("z", "c"), ("y", "x")), P(None, ("z", "c"), ("y", "x"), None))
    return jax.shard_map(
        body,
        mesh=grid,
        in_specs=placed,
        out_specs=(P(axes), P(axes), P()),
        check_vma=False,
    )
```

```python
import jax
import jax.numpy as jnp
from jax import lax
from jax.experimental import pallas as pl
from jax.experimental.pallas import tpu as pltpu
from jax.sharding import Mesh
from jax.sharding import PartitionSpec as P

D = 1024
ROWS_DEV = 256
ROUNDS = 3
CAP = 4
ROWS = 131072
NZ, NC, NY, NXA, NXI = 16, 2, 4, 2, 2
PLANE = NY * NXA * NXI
FAR = NY * NXA
NEAR = NC * NXI
BLK = 16
CNT_ROW = ROUNDS * CAP
KEEP = ROUNDS * NZ

VMEM = pltpu.VMEM
SMEM = pltpu.SMEM
F32 = jnp.float32
BF16 = jnp.bfloat16


def iota(shape, dim):
    return lax.broadcasted_iota(jnp.int32, shape, dim)


def one_hot(cond):
    return jnp.where(cond, 1.0, 0.0).astype(BF16)


def dot_nt(a, b):
    return lax.dot_general(a, b, (((1,), (1,)), ((), ())), preferred_element_type=F32)


def pack_kernel(cnt_hbm, idx_hbm, pts_hbm, out_ref, cnt_ref, idx_ref, pts_ref, sem):
    fetch_idx = pltpu.make_async_copy(idx_hbm, idx_ref, sem.at[0])
    fetch_cnt = pltpu.make_async_copy(cnt_hbm, cnt_ref, sem.at[1])
    fetch = pltpu.make_async_copy(pts_hbm, pts_ref, sem.at[2])
    fetch_idx.start()
    fetch_cnt.start()
    fetch.start()
    fetch_idx.wait()
    fetch_cnt.wait()
    sub = iota((BLK, ROWS_DEV), 0)
    lane = iota((BLK, ROWS_DEV), 1)
    want = jnp.full((BLK, ROWS_DEV), -1, jnp.int32)
    for q in range(CNT_ROW):
        want = jnp.where(sub == q, idx_ref[q // CAP, 0, 0, q % CAP], want)
    fetch.wait()
    rows = jnp.dot(one_hot(lane == want), pts_ref[...], preferred_element_type=F32)
    sub = iota((BLK, D), 0)
    lane = iota((BLK, D), 1)
    for r in range(ROUNDS):
        here = jnp.logical_and(sub == CNT_ROW, lane == r)
        rows = jnp.where(here, cnt_ref[r].astype(F32), rows)
    rows = rows.astype(BF16)
    for i in range(PLANE):
        out_ref[i] = rows


def compact_kernel(recv_ref, out_ref):
    place = (lax.axis_index("y") * NXA + lax.axis_index("xa")) * NXI + lax.axis_index("xi")
    n = PLANE * BLK
    head = recv_ref[:, 0:128]
    src = iota((n, n), 0)
    dst = iota((n, n), 1)
    is_cnt = src % BLK == CNT_ROW
    own = one_hot(jnp.logical_and(is_cnt, src // BLK == dst // BLK))
    before = one_hot(jnp.logical_and(is_cnt, src // BLK < dst // BLK))
    contract = (((0,), (0,)), ((), ()))
    cnt = lax.dot_general(head, own, contract, preferred_element_type=F32)[:16]
    off = lax.dot_general(head, before, contract, preferred_element_type=F32)[:16]
    r = iota((16, n), 0)
    q = iota((16, n), 1) % BLK
    j = (q % CAP).astype(F32)
    live = jnp.logical_and(q < CNT_ROW, q // CAP == r)
    live = jnp.logical_and(live, j < cnt)
    live = jnp.logical_and(live, off + j == place.astype(F32))
    rows = jnp.dot(one_hot(live), recv_ref[...], preferred_element_type=F32)
    rows = rows[0:4].astype(BF16)
    for i in range(NZ):
        out_ref[i] = rows


def spread_kernel(recv_ref, out_ref, tmp_ref):
    for z in range(NZ):
        tmp_ref[4 * z : 4 * z + 4, :] = recv_ref[z].astype(F32)
    m = iota((KEEP, 4 * NZ), 0)
    k = iota((KEEP, 4 * NZ), 1)
    sel = one_hot(k == 4 * (m % NZ) + m // NZ)
    rows = jnp.dot(sel, tmp_ref[...].astype(BF16), preferred_element_type=F32)
    rows = rows.astype(BF16)
    for i in range(FAR):
        out_ref[i] = rows


def base_kernel(pts_ref, center_ref, out_ref):
    pts = pts_ref[...]
    wide = pts.astype(F32)
    sq = wide * wide
    hi = sq.astype(BF16)
    lo = (sq - hi.astype(F32)).astype(BF16)
    ones = jnp.ones((16, D), BF16)
    rows_norm = (dot_nt(ones, hi) + dot_nt(ones, lo))[0:1]
    center = jnp.broadcast_to(center_ref[...].reshape(1, D), (16, D))
    cwide = center.astype(F32)
    cnorm = jnp.sum(cwide * cwide, axis=1, keepdims=True)
    first = (cnorm - 2.0 * dot_nt(center, pts))[0:1]
    out_ref[0:1] = rows_norm
    out_ref[1:2] = jnp.maximum(rows_norm + first, 0.0)


def near_kernel(base_ref, cands_ref, *refs):
    *pts_refs, out_ref = refs
    cands = cands_ref[...]
    wide = cands.astype(F32)
    norm = jnp.sum(wide * wide, axis=1, keepdims=True)
    core = lax.axis_index("c")
    side = lax.axis_index("xi")
    for k, pts_ref in enumerate(pts_refs):
        block = (core + k // NXI) % NC * NXI + (side + k % NXI) % NXI
        prod = dot_nt(cands, pts_ref[...])
        val = (norm - 2.0 * prod).reshape(FAR, ROUNDS, NZ, ROWS_DEV)
        least = jnp.min(jnp.min(val, axis=0), axis=1)
        tail = jnp.zeros((8 - ROUNDS, ROWS_DEV), F32)
        if k == 0:
            tail = jnp.concatenate([base_ref[0:2], tail[2:]], axis=0)
        rows = jnp.concatenate([least, tail], axis=0)
        for i in range(NEAR):
            out_ref[i, block] = rows


def last_kernel(recv_ref, run_ref, sums_ref, all_ref):
    def base_row(row):
        return jnp.concatenate([recv_ref[b, b, row : row + 1] for b in range(NEAR)], axis=0)

    rows_norm = base_row(ROUNDS)
    running = base_row(ROUNDS + 1)
    lane = iota((FAR, 128), 1)
    sums = jnp.where(lane == 0, jnp.sum(running), 0.0)
    for r in range(ROUNDS):
        least = recv_ref[0, :, r]
        for s in range(1, NEAR):
            least = jnp.minimum(least, recv_ref[s, :, r])
        running = jnp.minimum(running, jnp.maximum(rows_norm + least, 0.0))
        sums = jnp.where(lane == r + 1, jnp.sum(running), sums)
    for b in range(NEAR):
        all_ref[b] = running[b : b + 1]
    run_ref[...] = all_ref[lax.axis_index("c") * NXI + lax.axis_index("xi")]
    sums_ref[...] = sums


def relay_kernel(recv_ref, out_ref):
    total = jnp.sum(recv_ref[...], axis=0, keepdims=True)
    out_ref[...] = jnp.broadcast_to(total, (NZ, 128))


def final_kernel(recv_ref, run_ref, dist_ref, weight_ref, pot_ref):
    total = jnp.sum(recv_ref[...], axis=0, keepdims=True)
    lane = iota((1, 128), 1)
    last = jnp.sum(jnp.where(lane == ROUNDS, total, 0.0), axis=1, keepdims=True)
    running = run_ref[...]
    dist_ref[...] = running.reshape(ROWS_DEV)
    weight_ref[...] = (running * (ROWS / last)).reshape(ROWS_DEV)
    pot_ref[...] = total.reshape(128)[0 : ROUNDS + 1]


def vspec():
    return pl.BlockSpec(memory_space=VMEM)


def call(kernel, ins, outs, scratch=(), name=None, near=True):
    shapes = [VMEM(s, d) if near else jax.ShapeDtypeStruct(s, d) for s, d in outs]
    single = len(shapes) == 1
    kern = pl.pallas_call(
        kernel,
        in_specs=ins,
        out_specs=vspec() if single else [vspec() for _ in shapes],
        out_shape=shapes[0] if single else shapes,
        scratch_shapes=list(scratch),
        compiler_params=pltpu.CompilerParams(vmem_limit_bytes=16 << 20),
        name=name,
    )

    def run(*args):
        placed = []
        for a, i in zip(args, ins):
            space = VMEM if i.memory_space == VMEM else pltpu.HBM
            placed.append(pltpu.with_memory_space_constraint(a, space))
        return kern(*placed)

    return run


def body(points, first_center, counts, cand_index):
    pack = call(
        pack_kernel,
        [pl.BlockSpec(memory_space=pl.ANY)] * 3,
        [((PLANE, BLK, D), BF16)],
        [
            SMEM((ROUNDS,), jnp.int32),
            SMEM((ROUNDS, 1, 1, CAP), jnp.int32),
            VMEM((ROWS_DEV, D), BF16),
            pltpu.SemaphoreType.DMA((3,)),
        ],
        name="pack",
    )
    blocks = pack(counts.reshape(ROUNDS), cand_index, points)
    plane = ("y", "xa", "xi")
    far = ("y", "xa")
    blocks = lax.all_to_all(blocks, plane, 0, 0)
    compact = call(compact_kernel, [vspec()], [((NZ, 4, D), BF16)], name="compact")
    mine = compact(blocks.reshape(PLANE * BLK, D))
    mine, shared = lax.optimization_barrier((mine, points))
    mine = lax.all_to_all(mine, "z", 0, 0)

    def from_side(k):
        return lax.ppermute(shared, "xi", [((i + k) % NXI, i) for i in range(NXI)])

    here = [points] + [from_side(k) for k in range(1, NXI)]
    there = [lax.ppermute(p, "c", [(0, 1), (1, 0)]) for p in here]
    base = call(base_kernel, [vspec()] * 2, [((2, ROWS_DEV), F32)], name="base")(points, first_center)
    spread = call(spread_kernel, [vspec()], [((FAR, KEEP, D), BF16)], [VMEM((4 * NZ, D), F32)], name="spread")
    cands = lax.all_to_all(spread(mine), far, 0, 0).reshape(FAR * KEEP, D)
    near = call(near_kernel, [vspec()] * (2 + NEAR), [((NEAR, NEAR, 8, ROWS_DEV), F32)], name="near")
    mins = lax.all_to_all(near(base, cands, *here, *there), ("c", "xi"), 0, 0)
    last = call(
        last_kernel,
        [vspec()],
        [((1, ROWS_DEV), F32), ((FAR, 128), F32)],
        [VMEM((NEAR, 1, ROWS_DEV), F32)],
        name="last",
    )
    running, sums = last(mins)
    sums = lax.all_to_all(sums, far, 0, 0)
    relay = call(relay_kernel, [vspec()], [((NZ, 128), F32)], name="relay")
    sums = lax.all_to_all(relay(sums), "z", 0, 0)
    final = call(
        final_kernel,
        [vspec()] * 2,
        [((ROWS_DEV,), F32), ((ROWS_DEV,), F32), ((ROUNDS + 1,), F32)],
        name="final",
        near=False,
    )
    return tuple(final(sums, running))


def solution(mesh):
    axes = ("z", "c", "y", "xa", "xi")
    plane = ("y", "xa", "xi")
    grid = Mesh(mesh.devices.reshape(NZ, NC, NY, NXA, NXI), axes)
    placed = (P(axes, None), P(), P(None, ("z", "c"), plane), P(None, ("z", "c"), plane, None))
    return jax.shard_map(
        body,
        mesh=grid,
        in_specs=placed,
        out_specs=(P(axes), P(axes), P()),
        check_vma=False,
    )
```

```python
import jax
import jax.numpy as jnp
from jax import lax
from jax.experimental import pallas as pl
from jax.experimental.pallas import tpu as pltpu
from jax.sharding import Mesh
from jax.sharding import PartitionSpec as P


D = 1024
ROWS_DEV = 256
ROUNDS = 3
CAP = 4
ROWS = 131072
NZ, NC, NY, NXA, NXI = 16, 2, 4, 1, 4
PLANE = NY * NXA * NXI
FAR = NY * NXA
NEAR = NC * NXI
BLK = 16
CNT_ROW = ROUNDS * CAP
KEEP = ROUNDS * NZ

VMEM = pltpu.VMEM
SMEM = pltpu.SMEM
F32 = jnp.float32
BF16 = jnp.bfloat16


def iota(shape, dim):
    return lax.broadcasted_iota(jnp.int32, shape, dim)


def one_hot(cond):
    return jnp.where(cond, 1.0, 0.0).astype(BF16)


def dot_nt(a, b):
    return lax.dot_general(a, b, (((1,), (1,)), ((), ())), preferred_element_type=F32)


def pack_kernel(cnt_hbm, idx_hbm, pts_hbm, out_ref, cnt_ref, idx_ref, pts_ref, sem):
    fetch_idx = pltpu.make_async_copy(idx_hbm, idx_ref, sem.at[0])
    fetch_cnt = pltpu.make_async_copy(cnt_hbm, cnt_ref, sem.at[1])
    fetch = pltpu.make_async_copy(pts_hbm, pts_ref, sem.at[2])
    fetch_idx.start()
    fetch_cnt.start()
    fetch.start()
    fetch_idx.wait()
    fetch_cnt.wait()
    sub = iota((BLK, ROWS_DEV), 0)
    lane = iota((BLK, ROWS_DEV), 1)
    want = jnp.full((BLK, ROWS_DEV), -1, jnp.int32)
    for q in range(CNT_ROW):
        want = jnp.where(sub == q, idx_ref[q // CAP, 0, 0, q % CAP], want)
    fetch.wait()
    rows = jnp.dot(one_hot(lane == want), pts_ref[...], preferred_element_type=F32)
    sub = iota((BLK, D), 0)
    lane = iota((BLK, D), 1)
    for r in range(ROUNDS):
        here = jnp.logical_and(sub == CNT_ROW, lane == r)
        rows = jnp.where(here, cnt_ref[r].astype(F32), rows)
    rows = rows.astype(BF16)
    for i in range(PLANE):
        out_ref[i] = rows


def compact_kernel(recv_ref, out_ref):
    place = (lax.axis_index("y") * NXA + lax.axis_index("xa")) * NXI + lax.axis_index("xi")
    n = PLANE * BLK
    head = recv_ref[:, 0:128]
    src = iota((n, n), 0)
    dst = iota((n, n), 1)
    is_cnt = src % BLK == CNT_ROW
    own = one_hot(jnp.logical_and(is_cnt, src // BLK == dst // BLK))
    before = one_hot(jnp.logical_and(is_cnt, src // BLK < dst // BLK))
    contract = (((0,), (0,)), ((), ()))
    cnt = lax.dot_general(head, own, contract, preferred_element_type=F32)[:16]
    off = lax.dot_general(head, before, contract, preferred_element_type=F32)[:16]
    r = iota((16, n), 0)
    q = iota((16, n), 1) % BLK
    j = (q % CAP).astype(F32)
    live = jnp.logical_and(q < CNT_ROW, q // CAP == r)
    live = jnp.logical_and(live, j < cnt)
    live = jnp.logical_and(live, off + j == place.astype(F32))
    rows = jnp.dot(one_hot(live), recv_ref[...], preferred_element_type=F32)
    rows = rows[0:4].astype(BF16)
    for i in range(NZ):
        out_ref[i] = rows


def spread_kernel(recv_ref, out_ref, tmp_ref):
    for z in range(NZ):
        tmp_ref[4 * z : 4 * z + 4, :] = recv_ref[z].astype(F32)
    m = iota((KEEP, 4 * NZ), 0)
    k = iota((KEEP, 4 * NZ), 1)
    sel = one_hot(k == 4 * (m % NZ) + m // NZ)
    rows = jnp.dot(sel, tmp_ref[...].astype(BF16), preferred_element_type=F32)
    rows = rows.astype(BF16)
    for i in range(FAR):
        out_ref[i] = rows


def base_kernel(pts_ref, center_ref, out_ref):
    pts = pts_ref[...]
    wide = pts.astype(F32)
    sq = wide * wide
    hi = sq.astype(BF16)
    lo = (sq - hi.astype(F32)).astype(BF16)
    ones = jnp.ones((16, D), BF16)
    rows_norm = (dot_nt(ones, hi) + dot_nt(ones, lo))[0:1]
    center = jnp.broadcast_to(center_ref[...].reshape(1, D), (16, D))
    cwide = center.astype(F32)
    cnorm = jnp.sum(cwide * cwide, axis=1, keepdims=True)
    first = (cnorm - 2.0 * dot_nt(center, pts))[0:1]
    out_ref[0:1] = rows_norm
    out_ref[1:2] = jnp.maximum(rows_norm + first, 0.0)


def near_kernel(base_ref, cands_ref, *refs):
    *pts_refs, out_ref = refs
    cands = cands_ref[...]
    wide = cands.astype(F32)
    norm = jnp.sum(wide * wide, axis=1, keepdims=True)
    core = lax.axis_index("c")
    side = lax.axis_index("xi")
    for k, pts_ref in enumerate(pts_refs):
        block = (core + k // NXI) % NC * NXI + (side + k % NXI) % NXI
        prod = dot_nt(cands, pts_ref[...])
        val = (norm - 2.0 * prod).reshape(FAR, ROUNDS, NZ, ROWS_DEV)
        least = jnp.min(jnp.min(val, axis=0), axis=1)
        tail = jnp.zeros((8 - ROUNDS, ROWS_DEV), F32)
        if k == 0:
            tail = jnp.concatenate([base_ref[0:2], tail[2:]], axis=0)
        rows = jnp.concatenate([least, tail], axis=0)
        for i in range(NEAR):
            out_ref[i, block] = rows


def last_kernel(recv_ref, run_ref, sums_ref, all_ref):
    def base_row(row):
        return jnp.concatenate([recv_ref[b, b, row : row + 1] for b in range(NEAR)], axis=0)

    rows_norm = base_row(ROUNDS)
    running = base_row(ROUNDS + 1)
    lane = iota((FAR, 128), 1)
    sums = jnp.where(lane == 0, jnp.sum(running), 0.0)
    for r in range(ROUNDS):
        least = recv_ref[0, :, r]
        for s in range(1, NEAR):
            least = jnp.minimum(least, recv_ref[s, :, r])
        running = jnp.minimum(running, jnp.maximum(rows_norm + least, 0.0))
        sums = jnp.where(lane == r + 1, jnp.sum(running), sums)
    for b in range(NEAR):
        all_ref[b] = running[b : b + 1]
    run_ref[...] = all_ref[lax.axis_index("c") * NXI + lax.axis_index("xi")]
    sums_ref[...] = sums


def relay_kernel(recv_ref, out_ref):
    total = jnp.sum(recv_ref[...], axis=0, keepdims=True)
    out_ref[...] = jnp.broadcast_to(total, (NZ, 128))


def final_kernel(recv_ref, run_ref, dist_ref, weight_ref, pot_ref):
    total = jnp.sum(recv_ref[...], axis=0, keepdims=True)
    lane = iota((1, 128), 1)
    last = jnp.sum(jnp.where(lane == ROUNDS, total, 0.0), axis=1, keepdims=True)
    running = run_ref[...]
    dist_ref[...] = running.reshape(ROWS_DEV)
    weight_ref[...] = (running * (ROWS / last)).reshape(ROWS_DEV)
    pot_ref[...] = total.reshape(128)[0 : ROUNDS + 1]


def vspec():
    return pl.BlockSpec(memory_space=VMEM)


def call(kernel, ins, outs, scratch=(), near=True):
    shapes = [VMEM(s, d) if near else jax.ShapeDtypeStruct(s, d) for s, d in outs]
    single = len(shapes) == 1
    kern = pl.pallas_call(
        kernel,
        in_specs=ins,
        out_specs=vspec() if single else [vspec() for _ in shapes],
        out_shape=shapes[0] if single else shapes,
        scratch_shapes=list(scratch),
        compiler_params=pltpu.CompilerParams(vmem_limit_bytes=16 << 20),
    )

    def run(*args):
        placed = []
        for a, i in zip(args, ins):
            space = VMEM if i.memory_space == VMEM else pltpu.HBM
            placed.append(pltpu.with_memory_space_constraint(a, space))
        return kern(*placed)

    return run


def body(points, first_center, counts, cand_index):
    pack = call(
        pack_kernel,
        [pl.BlockSpec(memory_space=pl.ANY)] * 3,
        [((PLANE, BLK, D), BF16)],
        [
            SMEM((ROUNDS,), jnp.int32),
            SMEM((ROUNDS, 1, 1, CAP), jnp.int32),
            VMEM((ROWS_DEV, D), BF16),
            pltpu.SemaphoreType.DMA((3,)),
        ],
    )
    blocks = pack(counts.reshape(ROUNDS), cand_index, points)
    plane = ("y", "xa", "xi")
    far = ("y", "xa")
    blocks, early = lax.optimization_barrier((blocks, points))
    blocks = lax.all_to_all(blocks, plane, 0, 0)
    compact = call(compact_kernel, [vspec()], [((NZ, 4, D), BF16)])
    mine = compact(blocks.reshape(PLANE * BLK, D))
    mine, shared = lax.optimization_barrier((mine, points))
    mine = lax.all_to_all(mine, "z", 0, 0)

    def from_side(rows, k):
        return lax.ppermute(rows, "xi", [((i + k) % NXI, i) for i in range(NXI)])

    def swap(rows):
        return lax.ppermute(rows, "c", [(0, 1), (1, 0)])

    here = [points, from_side(early, 1), from_side(shared, 2), from_side(early, 3)]
    there = [swap(p) for p in here]
    base = call(base_kernel, [vspec()] * 2, [((2, ROWS_DEV), F32)])(points, first_center)
    spread = call(spread_kernel, [vspec()], [((FAR, KEEP, D), BF16)], [VMEM((4 * NZ, D), F32)])
    cands = lax.all_to_all(spread(mine), far, 0, 0).reshape(FAR * KEEP, D)
    near = call(near_kernel, [vspec()] * (2 + NEAR), [((NEAR, NEAR, 8, ROWS_DEV), F32)])
    mins = lax.all_to_all(near(base, cands, *here, *there), ("c", "xi"), 0, 0)
    last = call(
        last_kernel,
        [vspec()],
        [((1, ROWS_DEV), F32), ((FAR, 128), F32)],
        [VMEM((NEAR, 1, ROWS_DEV), F32)],
    )
    running, sums = last(mins)
    sums = lax.all_to_all(sums, far, 0, 0)
    relay = call(relay_kernel, [vspec()], [((NZ, 128), F32)])
    sums = lax.all_to_all(relay(sums), "z", 0, 0)
    final = call(
        final_kernel,
        [vspec()] * 2,
        [((ROWS_DEV,), F32), ((ROWS_DEV,), F32), ((ROUNDS + 1,), F32)],
        near=False,
    )
    return tuple(final(sums, running))


def solution(mesh):
    axes = ("z", "c", "y", "xa", "xi")
    plane = ("y", "xa", "xi")
    grid = Mesh(mesh.devices.reshape(NZ, NC, NY, NXA, NXI), axes)
    placed = (P(axes, None), P(), P(None, ("z", "c"), plane), P(None, ("z", "c"), plane, None))


    return jax.shard_map(
        body,
        mesh=grid,
        in_specs=placed,
        out_specs=(P(axes), P(axes), P()),
        check_vma=False,
    )
```

```python
import jax
import jax.numpy as jnp
from jax import lax
from jax.experimental import pallas as pl
from jax.experimental.pallas import tpu as pltpu
from jax.sharding import Mesh
from jax.sharding import PartitionSpec as P


D = 1024
ROWS_DEV = 256
ROUNDS = 3
CAP = 4
ROWS = 131072
NZ, NC, NY, NXA, NXI = 16, 2, 4, 1, 4
PLANE = NY * NXA * NXI
FAR = NY * NXA
NEAR = NC * NXI
BLK = 16
CNT_ROW = ROUNDS * CAP
KEEP = ROUNDS * NZ

VMEM = pltpu.VMEM
SMEM = pltpu.SMEM
F32 = jnp.float32
BF16 = jnp.bfloat16


def iota(shape, dim):
    return lax.broadcasted_iota(jnp.int32, shape, dim)


def one_hot(cond):
    return jnp.where(cond, 1.0, 0.0).astype(BF16)


def dot_nt(a, b):
    return lax.dot_general(a, b, (((1,), (1,)), ((), ())), preferred_element_type=F32)


def pack_kernel(cnt_hbm, idx_hbm, pts_hbm, out_ref, cnt_ref, idx_ref, pts_ref, sem):
    fetch_idx = pltpu.make_async_copy(idx_hbm, idx_ref, sem.at[0])
    fetch_cnt = pltpu.make_async_copy(cnt_hbm, cnt_ref, sem.at[1])
    fetch = pltpu.make_async_copy(pts_hbm, pts_ref, sem.at[2])
    fetch_idx.start()
    fetch_cnt.start()
    fetch.start()
    fetch_idx.wait()
    fetch_cnt.wait()
    sub = iota((BLK, ROWS_DEV), 0)
    lane = iota((BLK, ROWS_DEV), 1)
    want = jnp.full((BLK, ROWS_DEV), -1, jnp.int32)
    for q in range(CNT_ROW):
        want = jnp.where(sub == q, idx_ref[q // CAP, 0, 0, q % CAP], want)
    fetch.wait()
    rows = jnp.dot(one_hot(lane == want), pts_ref[...], preferred_element_type=F32)
    sub = iota((BLK, D), 0)
    lane = iota((BLK, D), 1)
    for r in range(ROUNDS):
        here = jnp.logical_and(sub == CNT_ROW, lane == r)
        rows = jnp.where(here, cnt_ref[r].astype(F32), rows)
    rows = rows.astype(BF16)
    for i in range(PLANE):
        out_ref[i] = rows


def compact_kernel(recv_ref, out_ref):
    place = (lax.axis_index("y") * NXA + lax.axis_index("xa")) * NXI + lax.axis_index("xi")
    n = PLANE * BLK
    head = recv_ref[:, 0:128]
    src = iota((n, n), 0)
    dst = iota((n, n), 1)
    is_cnt = src % BLK == CNT_ROW
    own = one_hot(jnp.logical_and(is_cnt, src // BLK == dst // BLK))
    before = one_hot(jnp.logical_and(is_cnt, src // BLK < dst // BLK))
    contract = (((0,), (0,)), ((), ()))
    cnt = lax.dot_general(head, own, contract, preferred_element_type=F32)[:16]
    off = lax.dot_general(head, before, contract, preferred_element_type=F32)[:16]
    r = iota((16, n), 0)
    q = iota((16, n), 1) % BLK
    j = (q % CAP).astype(F32)
    live = jnp.logical_and(q < CNT_ROW, q // CAP == r)
    live = jnp.logical_and(live, j < cnt)
    live = jnp.logical_and(live, off + j == place.astype(F32))
    rows = jnp.dot(one_hot(live), recv_ref[...], preferred_element_type=F32)
    rows = rows[0:4].astype(BF16)
    for i in range(NZ):
        out_ref[i] = rows


def spread_kernel(recv_ref, out_ref, tmp_ref):
    for z in range(NZ):
        tmp_ref[4 * z : 4 * z + 4, :] = recv_ref[z].astype(F32)
    m = iota((KEEP, 4 * NZ), 0)
    k = iota((KEEP, 4 * NZ), 1)
    sel = one_hot(k == 4 * (m % NZ) + m // NZ)
    rows = jnp.dot(sel, tmp_ref[...].astype(BF16), preferred_element_type=F32)
    rows = rows.astype(BF16)
    for i in range(FAR):
        out_ref[i] = rows


def base_kernel(pts_ref, center_ref, out_ref):
    pts = pts_ref[...]
    wide = pts.astype(F32)
    sq = wide * wide
    hi = sq.astype(BF16)
    lo = (sq - hi.astype(F32)).astype(BF16)
    ones = jnp.ones((16, D), BF16)
    rows_norm = (dot_nt(ones, hi) + dot_nt(ones, lo))[0:1]
    center = jnp.broadcast_to(center_ref[...].reshape(1, D), (16, D))
    cwide = center.astype(F32)
    cnorm = jnp.sum(cwide * cwide, axis=1, keepdims=True)
    first = (cnorm - 2.0 * dot_nt(center, pts))[0:1]
    out_ref[0:1] = rows_norm
    out_ref[1:2] = jnp.maximum(rows_norm + first, 0.0)


def near_kernel(base_ref, cands_ref, *refs):
    here = refs[:NXI]
    there = refs[NXI:NEAR]
    out_ref, got_ref, rows_ref, sem = refs[NEAR:]
    fetches = [pltpu.make_async_copy(src, got_ref.at[k], sem.at[k]) for k, src in enumerate(there)]
    for fetch in fetches:
        fetch.start()
    cands = cands_ref[...]
    wide = cands.astype(F32)
    norm = jnp.sum(wide * wide, axis=1, keepdims=True)
    core = lax.axis_index("c")
    side = lax.axis_index("xi")
    for k in range(NEAR):
        block = (core + k // NXI) % NC * NXI + (side + k % NXI) % NXI
        if k < NXI:
            pts = here[k][...]
        else:
            fetches[k - NXI].wait()
            pts = got_ref[k - NXI]
        val = (norm - 2.0 * dot_nt(cands, pts)).reshape(FAR, ROUNDS, NZ, ROWS_DEV)
        least = jnp.min(jnp.min(val, axis=0), axis=1)
        for r in range(ROUNDS):
            rows_ref[pl.ds(r * NEAR + block, 1), :] = least[r : r + 1]
    rows_ref[ROUNDS * NEAR : ROUNDS * NEAR + 2, :] = base_ref[...]
    rows_ref[ROUNDS * NEAR + 2 :, :] = jnp.zeros((NEAR - 2, ROWS_DEV), F32)
    rows = rows_ref[...]
    for i in range(NEAR):
        out_ref[i] = rows


def last_kernel(recv_ref, run_ref, sums_ref, all_ref):
    def base_row(row):
        row += ROUNDS * NEAR
        return jnp.concatenate([recv_ref[b, row : row + 1] for b in range(NEAR)], axis=0)

    rows_norm = base_row(0)
    running = base_row(1)
    lane = iota((FAR, 128), 1)
    sums = jnp.where(lane == 0, jnp.sum(running), 0.0)
    for r in range(ROUNDS):
        least = recv_ref[0, r * NEAR : (r + 1) * NEAR]
        for s in range(1, NEAR):
            least = jnp.minimum(least, recv_ref[s, r * NEAR : (r + 1) * NEAR])
        running = jnp.minimum(running, jnp.maximum(rows_norm + least, 0.0))
        sums = jnp.where(lane == r + 1, jnp.sum(running), sums)
    for b in range(NEAR):
        all_ref[b] = running[b : b + 1]
    run_ref[...] = all_ref[lax.axis_index("c") * NXI + lax.axis_index("xi")]
    sums_ref[...] = sums


def relay_kernel(recv_ref, out_ref):
    total = jnp.sum(recv_ref[...], axis=0, keepdims=True)
    out_ref[...] = jnp.broadcast_to(total, (NZ, 128))


def final_kernel(recv_ref, run_ref, dist_ref, weight_ref, pot_ref):
    total = jnp.sum(recv_ref[...], axis=0, keepdims=True)
    lane = iota((1, 128), 1)
    last = jnp.sum(jnp.where(lane == ROUNDS, total, 0.0), axis=1, keepdims=True)
    running = run_ref[...]
    dist_ref[...] = running.reshape(ROWS_DEV)
    weight_ref[...] = (running * (ROWS / last)).reshape(ROWS_DEV)
    pot_ref[...] = total.reshape(128)[0 : ROUNDS + 1]


def vspec():
    return pl.BlockSpec(memory_space=VMEM)


def call(kernel, ins, outs, scratch=(), near=True):
    shapes = [VMEM(s, d) if near else jax.ShapeDtypeStruct(s, d) for s, d in outs]
    single = len(shapes) == 1
    kern = pl.pallas_call(
        kernel,
        in_specs=ins,
        out_specs=vspec() if single else [vspec() for _ in shapes],
        out_shape=shapes[0] if single else shapes,
        scratch_shapes=list(scratch),
        compiler_params=pltpu.CompilerParams(vmem_limit_bytes=16 << 20),
    )

    def run(*args):
        placed = []
        for a, i in zip(args, ins):
            space = VMEM if i.memory_space == VMEM else pltpu.HBM
            placed.append(pltpu.with_memory_space_constraint(a, space))
        return kern(*placed)

    return run


def body(points, first_center, counts, cand_index):
    pack = call(
        pack_kernel,
        [pl.BlockSpec(memory_space=pl.ANY)] * 3,
        [((PLANE, BLK, D), BF16)],
        [
            SMEM((ROUNDS,), jnp.int32),
            SMEM((ROUNDS, 1, 1, CAP), jnp.int32),
            VMEM((ROWS_DEV, D), BF16),
            pltpu.SemaphoreType.DMA((3,)),
        ],
    )
    blocks = pack(counts.reshape(ROUNDS), cand_index, points)
    plane = ("y", "xa", "xi")
    far = ("y", "xa")
    blocks, early = lax.optimization_barrier((blocks, points))
    blocks = lax.all_to_all(blocks, plane, 0, 0)
    compact = call(compact_kernel, [vspec()], [((NZ, 4, D), BF16)])
    mine = compact(blocks.reshape(PLANE * BLK, D))
    mine, shared = lax.optimization_barrier((mine, points))
    mine = lax.all_to_all(mine, "z", 0, 0)

    def from_side(rows, k):
        return lax.ppermute(rows, "xi", [((i + k) % NXI, i) for i in range(NXI)])

    def swap(rows):
        return lax.ppermute(rows, "c", [(0, 1), (1, 0)])

    here = [points, from_side(early, 1), from_side(shared, 2), from_side(early, 3)]
    there = [swap(p) for p in here]
    base = call(base_kernel, [vspec()] * 2, [((2, ROWS_DEV), F32)])(points, first_center)
    spread = call(spread_kernel, [vspec()], [((FAR, KEEP, D), BF16)], [VMEM((4 * NZ, D), F32)])
    cands = lax.all_to_all(spread(mine), far, 0, 0).reshape(FAR * KEEP, D)
    near = call(
        near_kernel,
        [vspec()] * (2 + NXI) + [pl.BlockSpec(memory_space=pl.ANY)] * NXI,
        [((NEAR, 4 * NEAR, ROWS_DEV), F32)],
        [
            VMEM((NXI, ROWS_DEV, D), BF16),
            VMEM((4 * NEAR, ROWS_DEV), F32),
            pltpu.SemaphoreType.DMA((NXI,)),
        ],
    )
    mins = lax.all_to_all(near(base, cands, *here, *there), ("c", "xi"), 0, 0)
    last = call(
        last_kernel,
        [vspec()],
        [((1, ROWS_DEV), F32), ((FAR, 128), F32)],
        [VMEM((NEAR, 1, ROWS_DEV), F32)],
    )
    running, sums = last(mins)
    sums = lax.all_to_all(sums, far, 0, 0)
    relay = call(relay_kernel, [vspec()], [((NZ, 128), F32)])
    sums = lax.all_to_all(relay(sums), "z", 0, 0)
    final = call(
        final_kernel,
        [vspec()] * 2,
        [((ROWS_DEV,), F32), ((ROWS_DEV,), F32), ((ROUNDS + 1,), F32)],
        near=False,
    )
    return tuple(final(sums, running))


def solution(mesh):
    axes = ("z", "c", "y", "xa", "xi")
    plane = ("y", "xa", "xi")
    grid = Mesh(mesh.devices.reshape(NZ, NC, NY, NXA, NXI), axes)
    placed = (P(axes, None), P(), P(None, ("z", "c"), plane), P(None, ("z", "c"), plane, None))


    return jax.shard_map(
        body,
        mesh=grid,
        in_specs=placed,
        out_specs=(P(axes), P(axes), P()),
        check_vma=False,
    )
```

```python
import jax
import jax.numpy as jnp
from jax import lax
from jax.experimental import pallas as pl
from jax.experimental.pallas import tpu as pltpu
from jax.sharding import Mesh
from jax.sharding import PartitionSpec as P


D = 1024
ROWS_DEV = 256
ROUNDS = 3
CAP = 4
ROWS = 131072
NZ, NC, NY, NX = 16, 2, 4, 4
PLANE = NY * NX
FAR = NC * NY
NEAR = NX
BLK = 16
CNT_ROW = ROUNDS * CAP
KEEP = ROUNDS * NZ

VMEM = pltpu.VMEM
SMEM = pltpu.SMEM
F32 = jnp.float32
BF16 = jnp.bfloat16


def iota(shape, dim):
    return lax.broadcasted_iota(jnp.int32, shape, dim)


def one_hot(cond):
    return jnp.where(cond, 1.0, 0.0).astype(BF16)


def dot_nt(a, b):
    return lax.dot_general(a, b, (((1,), (1,)), ((), ())), preferred_element_type=F32)


def pack_kernel(cnt_hbm, idx_hbm, pts_hbm, out_ref, cnt_ref, idx_ref, pts_ref, sem):
    fetch_idx = pltpu.make_async_copy(idx_hbm, idx_ref, sem.at[0])
    fetch_cnt = pltpu.make_async_copy(cnt_hbm, cnt_ref, sem.at[1])
    fetch = pltpu.make_async_copy(pts_hbm, pts_ref, sem.at[2])
    fetch_idx.start()
    fetch_cnt.start()
    fetch.start()
    fetch_idx.wait()
    fetch_cnt.wait()
    sub = iota((BLK, ROWS_DEV), 0)
    lane = iota((BLK, ROWS_DEV), 1)
    want = jnp.full((BLK, ROWS_DEV), -1, jnp.int32)
    for q in range(CNT_ROW):
        want = jnp.where(sub == q, idx_ref[q // CAP, 0, 0, q % CAP], want)
    fetch.wait()
    rows = jnp.dot(one_hot(lane == want), pts_ref[...], preferred_element_type=F32)
    sub = iota((BLK, D), 0)
    lane = iota((BLK, D), 1)
    for r in range(ROUNDS):
        here = jnp.logical_and(sub == CNT_ROW, lane == r)
        rows = jnp.where(here, cnt_ref[r].astype(F32), rows)
    rows = rows.astype(BF16)
    for i in range(PLANE):
        out_ref[i] = rows


def compact_kernel(recv_ref, out_ref):
    place = lax.axis_index("y") * NX + lax.axis_index("x")
    n = PLANE * BLK
    head = recv_ref[:, 0:128]
    src = iota((n, n), 0)
    dst = iota((n, n), 1)
    is_cnt = src % BLK == CNT_ROW
    own = one_hot(jnp.logical_and(is_cnt, src // BLK == dst // BLK))
    before = one_hot(jnp.logical_and(is_cnt, src // BLK < dst // BLK))
    contract = (((0,), (0,)), ((), ()))
    cnt = lax.dot_general(head, own, contract, preferred_element_type=F32)[:16]
    off = lax.dot_general(head, before, contract, preferred_element_type=F32)[:16]
    r = iota((16, n), 0)
    q = iota((16, n), 1) % BLK
    j = (q % CAP).astype(F32)
    live = jnp.logical_and(q < CNT_ROW, q // CAP == r)
    live = jnp.logical_and(live, j < cnt)
    live = jnp.logical_and(live, off + j == place.astype(F32))
    rows = jnp.dot(one_hot(live), recv_ref[...], preferred_element_type=F32)
    rows = rows[0:4].astype(BF16)
    for i in range(NZ):
        out_ref[i] = rows


def spread_kernel(recv_ref, out_ref, tmp_ref):
    for z in range(NZ):
        tmp_ref[4 * z : 4 * z + 4, :] = recv_ref[z].astype(F32)
    m = iota((KEEP, 4 * NZ), 0)
    k = iota((KEEP, 4 * NZ), 1)
    sel = one_hot(k == 4 * (m % NZ) + m // NZ)
    rows = jnp.dot(sel, tmp_ref[...].astype(BF16), preferred_element_type=F32)
    rows = rows.astype(BF16)
    for i in range(FAR):
        out_ref[i] = rows


def base_kernel(pts_ref, center_ref, out_ref):
    pts = pts_ref[...]
    wide = pts.astype(F32)
    sq = wide * wide
    hi = sq.astype(BF16)
    lo = (sq - hi.astype(F32)).astype(BF16)
    ones = jnp.ones((16, D), BF16)
    rows_norm = (dot_nt(ones, hi) + dot_nt(ones, lo))[0:1]
    center = jnp.broadcast_to(center_ref[...].reshape(1, D), (16, D))
    cwide = center.astype(F32)
    cnorm = jnp.sum(cwide * cwide, axis=1, keepdims=True)
    first = (cnorm - 2.0 * dot_nt(center, pts))[0:1]
    out_ref[0:1] = rows_norm
    out_ref[1:2] = jnp.maximum(rows_norm + first, 0.0)


def near_kernel(base_ref, cands_ref, *refs):
    *pts_refs, out_ref, rows_ref = refs
    cands = cands_ref[...]
    wide = cands.astype(F32)
    norm = jnp.sum(wide * wide, axis=1, keepdims=True)
    place = lax.axis_index("x")
    for k, pts_ref in enumerate(pts_refs):
        block = (place + k) % NEAR
        val = (norm - 2.0 * dot_nt(cands, pts_ref[...])).reshape(FAR, ROUNDS, NZ, ROWS_DEV)
        least = jnp.min(jnp.min(val, axis=0), axis=1)
        for r in range(ROUNDS):
            rows_ref[pl.ds(r * NEAR + block, 1), :] = least[r : r + 1]
    rows_ref[ROUNDS * NEAR : ROUNDS * NEAR + 2, :] = base_ref[...]
    rows_ref[ROUNDS * NEAR + 2 :, :] = jnp.zeros((NEAR - 2, ROWS_DEV), F32)
    rows = rows_ref[...]
    for i in range(NEAR):
        out_ref[i] = rows


def last_kernel(recv_ref, run_ref, sums_ref, all_ref):
    def base_row(row):
        row += ROUNDS * NEAR
        return jnp.concatenate([recv_ref[b, row : row + 1] for b in range(NEAR)], axis=0)

    rows_norm = base_row(0)
    running = base_row(1)
    lane = iota((FAR, 128), 1)
    sums = jnp.where(lane == 0, jnp.sum(running), 0.0)
    for r in range(ROUNDS):
        least = recv_ref[0, r * NEAR : (r + 1) * NEAR]
        for s in range(1, NEAR):
            least = jnp.minimum(least, recv_ref[s, r * NEAR : (r + 1) * NEAR])
        running = jnp.minimum(running, jnp.maximum(rows_norm + least, 0.0))
        sums = jnp.where(lane == r + 1, jnp.sum(running), sums)
    for b in range(NEAR):
        all_ref[b] = running[b : b + 1]
    run_ref[...] = all_ref[lax.axis_index("x")]
    sums_ref[...] = sums


def relay_kernel(recv_ref, out_ref):
    total = jnp.sum(recv_ref[...], axis=0, keepdims=True)
    out_ref[...] = jnp.broadcast_to(total, (NZ, 128))


def final_kernel(recv_ref, run_ref, dist_ref, weight_ref, pot_ref):
    total = jnp.sum(recv_ref[...], axis=0, keepdims=True)
    lane = iota((1, 128), 1)
    last = jnp.sum(jnp.where(lane == ROUNDS, total, 0.0), axis=1, keepdims=True)
    running = run_ref[...]
    dist_ref[...] = running.reshape(ROWS_DEV)
    weight_ref[...] = (running * (ROWS / last)).reshape(ROWS_DEV)
    pot_ref[...] = total.reshape(128)[0 : ROUNDS + 1]


def vspec():
    return pl.BlockSpec(memory_space=VMEM)


def call(kernel, ins, outs, scratch=(), near=True):
    shapes = [VMEM(s, d) if near else jax.ShapeDtypeStruct(s, d) for s, d in outs]
    single = len(shapes) == 1
    kern = pl.pallas_call(
        kernel,
        in_specs=ins,
        out_specs=vspec() if single else [vspec() for _ in shapes],
        out_shape=shapes[0] if single else shapes,
        scratch_shapes=list(scratch),
        compiler_params=pltpu.CompilerParams(vmem_limit_bytes=16 << 20),
    )

    def run(*args):
        placed = []
        for a, i in zip(args, ins):
            space = VMEM if i.memory_space == VMEM else pltpu.HBM
            placed.append(pltpu.with_memory_space_constraint(a, space))
        return kern(*placed)

    return run


def body(points, first_center, counts, cand_index):
    pack = call(
        pack_kernel,
        [pl.BlockSpec(memory_space=pl.ANY)] * 3,
        [((PLANE, BLK, D), BF16)],
        [
            SMEM((ROUNDS,), jnp.int32),
            SMEM((ROUNDS, 1, 1, CAP), jnp.int32),
            VMEM((ROWS_DEV, D), BF16),
            pltpu.SemaphoreType.DMA((3,)),
        ],
    )
    blocks = pack(counts.reshape(ROUNDS), cand_index, points)
    plane = ("y", "x")
    far = ("c", "y")
    blocks, early = lax.optimization_barrier((blocks, points))
    blocks = lax.all_to_all(blocks, plane, 0, 0)
    compact = call(compact_kernel, [vspec()], [((NZ, 4, D), BF16)])
    mine = compact(blocks.reshape(PLANE * BLK, D))
    mine, shared = lax.optimization_barrier((mine, points))
    mine = lax.all_to_all(mine, "z", 0, 0)

    def from_side(rows, k):
        return lax.ppermute(rows, "x", [((i + k) % NX, i) for i in range(NX)])

    line = [points, from_side(early, 1), from_side(shared, 2), from_side(early, 3)]
    base = call(base_kernel, [vspec()] * 2, [((2, ROWS_DEV), F32)])(points, first_center)
    spread = call(spread_kernel, [vspec()], [((FAR, KEEP, D), BF16)], [VMEM((4 * NZ, D), F32)])
    cands = lax.all_to_all(spread(mine), far, 0, 0).reshape(FAR * KEEP, D)
    near = call(
        near_kernel,
        [vspec()] * (2 + NEAR),
        [((NEAR, 4 * NEAR, ROWS_DEV), F32)],
        [VMEM((4 * NEAR, ROWS_DEV), F32)],
    )
    mins = lax.all_to_all(near(base, cands, *line), "x", 0, 0)
    last = call(
        last_kernel,
        [vspec()],
        [((1, ROWS_DEV), F32), ((FAR, 128), F32)],
        [VMEM((NEAR, 1, ROWS_DEV), F32)],
    )
    running, sums = last(mins)
    sums = lax.all_to_all(sums, far, 0, 0)
    relay = call(relay_kernel, [vspec()], [((NZ, 128), F32)])
    sums = lax.all_to_all(relay(sums), "z", 0, 0)
    final = call(
        final_kernel,
        [vspec()] * 2,
        [((ROWS_DEV,), F32), ((ROWS_DEV,), F32), ((ROUNDS + 1,), F32)],
        near=False,
    )
    return tuple(final(sums, running))


def solution(mesh):
    axes = ("z", "c", "y", "x")
    grid = Mesh(mesh.devices.reshape(NZ, NC, NY, NX), axes)
    placed = (P(axes, None), P(), P(None, ("z", "c"), ("y", "x")), P(None, ("z", "c"), ("y", "x"), None))

    return jax.shard_map(
        body,
        mesh=grid,
        in_specs=placed,
        out_specs=(P(axes), P(axes), P()),
        check_vma=False,
    )
```

```python
import jax
import jax.numpy as jnp
from jax import lax
from jax.experimental import pallas as pl
from jax.experimental.pallas import tpu as pltpu
from jax.sharding import Mesh
from jax.sharding import PartitionSpec as P


D = 1024
ROWS_DEV = 256
ROUNDS = 3
CAP = 4
ROWS = 131072
NZ, NC, NY, NX = 16, 2, 4, 4
PLANE = NY * NX
FAR = NY
NEAR = NX
BLK = 16
CNT_ROW = ROUNDS * CAP
KEEP = ROUNDS * NZ

VMEM = pltpu.VMEM
SMEM = pltpu.SMEM
F32 = jnp.float32
BF16 = jnp.bfloat16


def iota(shape, dim):
    return lax.broadcasted_iota(jnp.int32, shape, dim)


def one_hot(cond):
    return jnp.where(cond, 1.0, 0.0).astype(BF16)


def dot_nt(a, b):
    return lax.dot_general(a, b, (((1,), (1,)), ((), ())), preferred_element_type=F32)


def pack_kernel(cnt_hbm, idx_hbm, pts_hbm, out_ref, cnt_ref, idx_ref, pts_ref, sem):
    fetch_idx = pltpu.make_async_copy(idx_hbm, idx_ref, sem.at[0])
    fetch_cnt = pltpu.make_async_copy(cnt_hbm, cnt_ref, sem.at[1])
    fetch = pltpu.make_async_copy(pts_hbm, pts_ref, sem.at[2])
    fetch_idx.start()
    fetch_cnt.start()
    fetch.start()
    fetch_idx.wait()
    fetch_cnt.wait()
    sub = iota((BLK, ROWS_DEV), 0)
    lane = iota((BLK, ROWS_DEV), 1)
    want = jnp.full((BLK, ROWS_DEV), -1, jnp.int32)
    for q in range(CNT_ROW):
        want = jnp.where(sub == q, idx_ref[q // CAP, 0, 0, q % CAP], want)
    fetch.wait()
    rows = jnp.dot(one_hot(lane == want), pts_ref[...], preferred_element_type=F32)
    sub = iota((BLK, D), 0)
    lane = iota((BLK, D), 1)
    for r in range(ROUNDS):
        here = jnp.logical_and(sub == CNT_ROW, lane == r)
        rows = jnp.where(here, cnt_ref[r].astype(F32), rows)
    rows = rows.astype(BF16)
    for i in range(PLANE):
        out_ref[i] = rows


def compact_kernel(recv_ref, out_ref):
    place = lax.axis_index("y") * NX + lax.axis_index("x")
    n = PLANE * BLK
    head = recv_ref[:, 0:128]
    src = iota((n, n), 0)
    dst = iota((n, n), 1)
    is_cnt = src % BLK == CNT_ROW
    own = one_hot(jnp.logical_and(is_cnt, src // BLK == dst // BLK))
    before = one_hot(jnp.logical_and(is_cnt, src // BLK < dst // BLK))
    contract = (((0,), (0,)), ((), ()))
    cnt = lax.dot_general(head, own, contract, preferred_element_type=F32)[:16]
    off = lax.dot_general(head, before, contract, preferred_element_type=F32)[:16]
    r = iota((16, n), 0)
    q = iota((16, n), 1) % BLK
    j = (q % CAP).astype(F32)
    live = jnp.logical_and(q < CNT_ROW, q // CAP == r)
    live = jnp.logical_and(live, j < cnt)
    live = jnp.logical_and(live, off + j == place.astype(F32))
    rows = jnp.dot(one_hot(live), recv_ref[...], preferred_element_type=F32)
    rows = rows[0:4].astype(BF16)
    for i in range(NZ):
        out_ref[i] = rows


def spread_kernel(recv_ref, out_ref, tmp_ref):
    for z in range(NZ):
        tmp_ref[4 * z : 4 * z + 4, :] = recv_ref[z].astype(F32)
    m = iota((KEEP, 4 * NZ), 0)
    k = iota((KEEP, 4 * NZ), 1)
    sel = one_hot(k == 4 * (m % NZ) + m // NZ)
    rows = jnp.dot(sel, tmp_ref[...].astype(BF16), preferred_element_type=F32)
    rows = rows.astype(BF16)
    for i in range(FAR):
        out_ref[i] = rows


def base_kernel(pts_ref, center_ref, out_ref):
    pts = pts_ref[...]
    wide = pts.astype(F32)
    sq = wide * wide
    hi = sq.astype(BF16)
    lo = (sq - hi.astype(F32)).astype(BF16)
    ones = jnp.ones((16, D), BF16)
    rows_norm = (dot_nt(ones, hi) + dot_nt(ones, lo))[0:1]
    center = jnp.broadcast_to(center_ref[...].reshape(1, D), (16, D))
    cwide = center.astype(F32)
    cnorm = jnp.sum(cwide * cwide, axis=1, keepdims=True)
    first = (cnorm - 2.0 * dot_nt(center, pts))[0:1]
    out_ref[0:1] = rows_norm
    out_ref[1:2] = jnp.maximum(rows_norm + first, 0.0)


def line_mins(cands_ref, pts_refs, rows_ref):
    cands = cands_ref[...]
    wide = cands.astype(F32)
    norm = jnp.sum(wide * wide, axis=1, keepdims=True)
    place = lax.axis_index("x")
    for k, pts_ref in enumerate(pts_refs):
        block = (place + k) % NEAR
        val = (norm - 2.0 * dot_nt(cands, pts_ref[...])).reshape(FAR, ROUNDS, NZ, ROWS_DEV)
        least = jnp.min(jnp.min(val, axis=0), axis=1)
        for r in range(ROUNDS):
            rows_ref[pl.ds(r * NEAR + block, 1), :] = least[r : r + 1]


def own_kernel(base_ref, cands_ref, *refs):
    *pts_refs, rows_ref = refs
    rows_ref[ROUNDS * NEAR : ROUNDS * NEAR + 2, :] = base_ref[...]
    rows_ref[ROUNDS * NEAR + 2 :, :] = jnp.zeros((NEAR - 2, ROWS_DEV), F32)
    line_mins(cands_ref, pts_refs, rows_ref)


def other_kernel(own_ref, cands_ref, *refs):
    *pts_refs, out_ref, rows_ref = refs
    rows_ref[...] = own_ref[...]
    line_mins(cands_ref, pts_refs, rows_ref)
    rows = jnp.minimum(rows_ref[...], own_ref[...])
    for i in range(NEAR):
        out_ref[i] = rows


def last_kernel(recv_ref, run_ref, sums_ref, all_ref):
    def base_row(row):
        row += ROUNDS * NEAR
        return jnp.concatenate([recv_ref[b, row : row + 1] for b in range(NEAR)], axis=0)

    rows_norm = base_row(0)
    running = base_row(1)
    lane = iota((NC * FAR, 128), 1)
    sums = jnp.where(lane == 0, jnp.sum(running), 0.0)
    for r in range(ROUNDS):
        least = recv_ref[0, r * NEAR : (r + 1) * NEAR]
        for s in range(1, NEAR):
            least = jnp.minimum(least, recv_ref[s, r * NEAR : (r + 1) * NEAR])
        running = jnp.minimum(running, jnp.maximum(rows_norm + least, 0.0))
        sums = jnp.where(lane == r + 1, jnp.sum(running), sums)
    for b in range(NEAR):
        all_ref[b] = running[b : b + 1]
    run_ref[...] = all_ref[lax.axis_index("x")]
    sums_ref[...] = sums


def relay_kernel(recv_ref, out_ref):
    total = jnp.sum(recv_ref[...], axis=0, keepdims=True)
    out_ref[...] = jnp.broadcast_to(total, (NZ, 128))


def final_kernel(recv_ref, run_ref, dist_ref, weight_ref, pot_ref):
    total = jnp.sum(recv_ref[...], axis=0, keepdims=True)
    lane = iota((1, 128), 1)
    last = jnp.sum(jnp.where(lane == ROUNDS, total, 0.0), axis=1, keepdims=True)
    running = run_ref[...]
    dist_ref[...] = running.reshape(ROWS_DEV)
    weight_ref[...] = (running * (ROWS / last)).reshape(ROWS_DEV)
    pot_ref[...] = total.reshape(128)[0 : ROUNDS + 1]


def vspec():
    return pl.BlockSpec(memory_space=VMEM)


def call(kernel, ins, outs, scratch=(), near=True):
    shapes = [VMEM(s, d) if near else jax.ShapeDtypeStruct(s, d) for s, d in outs]
    single = len(shapes) == 1
    kern = pl.pallas_call(
        kernel,
        in_specs=ins,
        out_specs=vspec() if single else [vspec() for _ in shapes],
        out_shape=shapes[0] if single else shapes,
        scratch_shapes=list(scratch),
        compiler_params=pltpu.CompilerParams(vmem_limit_bytes=16 << 20),
    )

    def run(*args):
        placed = []
        for a, i in zip(args, ins):
            space = VMEM if i.memory_space == VMEM else pltpu.HBM
            placed.append(pltpu.with_memory_space_constraint(a, space))
        return kern(*placed)

    return run


def body(points, first_center, counts, cand_index):
    pack = call(
        pack_kernel,
        [pl.BlockSpec(memory_space=pl.ANY)] * 3,
        [((PLANE, BLK, D), BF16)],
        [
            SMEM((ROUNDS,), jnp.int32),
            SMEM((ROUNDS, 1, 1, CAP), jnp.int32),
            VMEM((ROWS_DEV, D), BF16),
            pltpu.SemaphoreType.DMA((3,)),
        ],
    )
    blocks = pack(counts.reshape(ROUNDS), cand_index, points)
    plane = ("y", "x")
    blocks, early = lax.optimization_barrier((blocks, points))
    blocks = lax.all_to_all(blocks, plane, 0, 0)
    compact = call(compact_kernel, [vspec()], [((NZ, 4, D), BF16)])
    mine = compact(blocks.reshape(PLANE * BLK, D))
    mine, shared = lax.optimization_barrier((mine, points))
    mine = lax.all_to_all(mine, "z", 0, 0)

    def from_side(rows, k):
        return lax.ppermute(rows, "x", [((i + k) % NX, i) for i in range(NX)])

    line = [points, from_side(early, 1), from_side(shared, 2), from_side(early, 3)]
    base = call(base_kernel, [vspec()] * 2, [((2, ROWS_DEV), F32)])(points, first_center)
    spread = call(spread_kernel, [vspec()], [((FAR, KEEP, D), BF16)], [VMEM((4 * NZ, D), F32)])
    cands = lax.all_to_all(spread(mine), "y", 0, 0).reshape(FAR * KEEP, D)
    others = lax.ppermute(cands, "c", [(0, 1), (1, 0)])
    rows = ((4 * NEAR, ROWS_DEV), F32)
    own = call(own_kernel, [vspec()] * (2 + NEAR), [rows])
    other = call(other_kernel, [vspec()] * (2 + NEAR), [((NEAR, *rows[0]), F32)], [VMEM(*rows)])
    mins = lax.all_to_all(other(own(base, cands, *line), others, *line), "x", 0, 0)
    last = call(
        last_kernel,
        [vspec()],
        [((1, ROWS_DEV), F32), ((NC * FAR, 128), F32)],
        [VMEM((NEAR, 1, ROWS_DEV), F32)],
    )
    running, sums = last(mins)
    sums = lax.all_to_all(sums, ("c", "y"), 0, 0)
    relay = call(relay_kernel, [vspec()], [((NZ, 128), F32)])
    sums = lax.all_to_all(relay(sums), "z", 0, 0)
    final = call(
        final_kernel,
        [vspec()] * 2,
        [((ROWS_DEV,), F32), ((ROWS_DEV,), F32), ((ROUNDS + 1,), F32)],
        near=False,
    )
    return tuple(final(sums, running))


def solution(mesh):
    axes = ("z", "c", "y", "x")
    grid = Mesh(mesh.devices.reshape(NZ, NC, NY, NX), axes)
    placed = (P(axes, None), P(), P(None, ("z", "c"), ("y", "x")), P(None, ("z", "c"), ("y", "x"), None))

    return jax.shard_map(
        body,
        mesh=grid,
        in_specs=placed,
        out_specs=(P(axes), P(axes), P()),
        check_vma=False,
    )
```

```python
import jax
import jax.numpy as jnp
from jax import lax
from jax.experimental import pallas as pl
from jax.experimental.pallas import tpu as pltpu
from jax.sharding import Mesh
from jax.sharding import PartitionSpec as P


D = 1024
ROWS_DEV = 256
ROUNDS = 3
CAP = 4
ROWS = 131072
NZ, NC, NY, NX = 16, 2, 4, 4
PLANE = NY * NX
FAR = NY
NEAR = NX
SLOTS = ROUNDS * CAP
LANES = 128
FOLD = D // LANES
KEEP = ROUNDS * NZ

VMEM = pltpu.VMEM
SMEM = pltpu.SMEM
F32 = jnp.float32
BF16 = jnp.bfloat16


def iota(shape, dim):
    return lax.broadcasted_iota(jnp.int32, shape, dim)


def one_hot(cond):
    return jnp.where(cond, 1.0, 0.0).astype(BF16)


def dot_nt(a, b):
    return lax.dot_general(a, b, (((1,), (1,)), ((), ())), preferred_element_type=F32)


def pack_kernel(cnt_hbm, idx_hbm, pts_hbm, out_ref, cnt_ref, idx_ref, pts_ref, sem):
    fetch_idx = pltpu.make_async_copy(idx_hbm, idx_ref, sem.at[0])
    fetch_cnt = pltpu.make_async_copy(cnt_hbm, cnt_ref, sem.at[1])
    fetch = pltpu.make_async_copy(pts_hbm, pts_ref, sem.at[2])
    fetch_idx.start()
    fetch_cnt.start()
    fetch.start()
    fetch_idx.wait()
    fetch_cnt.wait()
    sub = iota((16, ROWS_DEV), 0)
    lane = iota((16, ROWS_DEV), 1)
    want = jnp.full((16, ROWS_DEV), -1, jnp.int32)
    for q in range(SLOTS):
        r, j = divmod(q, CAP)
        row = jnp.where(j < cnt_ref[r], idx_ref[r, 0, 0, j], -1)
        want = jnp.where(sub == q, row, want)
    fetch.wait()
    rows = jnp.dot(one_hot(lane == want), pts_ref[...], preferred_element_type=F32)
    dead = jnp.logical_and(want < 0, lane == 0)[:, :LANES]
    head = jnp.where(dead, jnp.inf, rows[:, :LANES]).astype(BF16)
    tail = rows[:, LANES:].astype(BF16)
    for i in range(PLANE):
        for r in range(ROUNDS):
            out_ref[i, r, :, :LANES] = head[r * CAP : (r + 1) * CAP]
            out_ref[i, r, :, LANES:] = tail[r * CAP : (r + 1) * CAP]


def compact_kernel(recv_ref, out_ref, tmp_ref, fold_ref):
    place = lax.axis_index("y") * NX + lax.axis_index("x")
    n = PLANE * SLOTS
    for s in range(PLANE):
        for r in range(ROUNDS):
            at = s * SLOTS + r * CAP
            tmp_ref[at : at + CAP, :] = recv_ref[s, r].astype(F32)
    head = tmp_ref[:, :LANES]
    dead = head == jnp.inf
    live = one_hot(jnp.logical_not(dead))
    src = iota((n, n), 0)
    dst = iota((n, n), 1)
    same = src % SLOTS // CAP == dst % SLOTS // CAP
    before = one_hot(jnp.logical_and(same, src < dst))
    here = one_hot(src == dst)
    contract = (((0,), (0,)), ((), ()))
    pos = lax.dot_general(live, before, contract, preferred_element_type=F32)[0:1]
    alive = lax.dot_general(live, here, contract, preferred_element_type=F32)[0:1]
    slot = jnp.where(alive > 0.5, pos, -1.0)
    round_of = iota((16, n), 1) % SLOTS // CAP
    take = jnp.logical_and(round_of == iota((16, n), 0), slot == place.astype(F32))
    take = one_hot(take)
    head = jnp.where(dead, 0.0, head).astype(BF16)
    head = jnp.dot(take, head, preferred_element_type=F32)
    tail = jnp.dot(take, tmp_ref[:, LANES:].astype(BF16), preferred_element_type=F32)
    rows = jnp.concatenate([head, tail], axis=1)
    for r in range(ROUNDS):
        for f in range(FOLD):
            at = r * FOLD + f
            fold_ref[at : at + 1, :] = rows[r : r + 1, f * LANES : (f + 1) * LANES]
    block = fold_ref[...].astype(BF16)
    for i in range(NZ):
        out_ref[i] = block


def spread_kernel(recv_ref, out_ref):
    n = NZ * ROUNDS * FOLD
    m = iota((n, n), 0)
    k = iota((n, n), 1)
    z = m % NZ
    r = m // NZ % ROUNDS
    f = m // KEEP
    sel = one_hot(k == (z * ROUNDS + r) * FOLD + f)
    parts = jnp.dot(sel, recv_ref[...], preferred_element_type=F32).astype(BF16)
    for i in range(FAR):
        for f in range(FOLD):
            out_ref[i, :, f * LANES : (f + 1) * LANES] = parts[f * KEEP : (f + 1) * KEEP]


def base_kernel(pts_ref, center_ref, out_ref):
    pts = pts_ref[...]
    wide = pts.astype(F32)
    sq = wide * wide
    hi = sq.astype(BF16)
    lo = (sq - hi.astype(F32)).astype(BF16)
    ones = jnp.ones((16, D), BF16)
    rows_norm = (dot_nt(ones, hi) + dot_nt(ones, lo))[0:1]
    center = jnp.broadcast_to(center_ref[...].reshape(1, D), (16, D))
    cwide = center.astype(F32)
    cnorm = jnp.sum(cwide * cwide, axis=1, keepdims=True)
    first = (cnorm - 2.0 * dot_nt(center, pts))[0:1]
    out_ref[0:1] = rows_norm
    out_ref[1:2] = jnp.maximum(rows_norm + first, 0.0)


def line_mins(cands_ref, pts_refs, rows_ref):
    cands = cands_ref[...]
    wide = cands.astype(F32)
    norm = jnp.sum(wide * wide, axis=1, keepdims=True)
    place = lax.axis_index("x")
    for k, pts_ref in enumerate(pts_refs):
        block = (place + k) % NEAR
        val = (norm - 2.0 * dot_nt(cands, pts_ref[...])).reshape(FAR, ROUNDS, NZ, ROWS_DEV)
        least = jnp.min(jnp.min(val, axis=0), axis=1)
        for r in range(ROUNDS):
            rows_ref[pl.ds(r * NEAR + block, 1), :] = least[r : r + 1]


def own_kernel(base_ref, cands_ref, *refs):
    *pts_refs, rows_ref = refs
    rows_ref[ROUNDS * NEAR : ROUNDS * NEAR + 2, :] = base_ref[...]
    rows_ref[ROUNDS * NEAR + 2 :, :] = jnp.zeros((NEAR - 2, ROWS_DEV), F32)
    line_mins(cands_ref, pts_refs, rows_ref)


def other_kernel(own_ref, cands_ref, *refs):
    *pts_refs, out_ref, rows_ref = refs
    rows_ref[...] = own_ref[...]
    line_mins(cands_ref, pts_refs, rows_ref)
    rows = jnp.minimum(rows_ref[...], own_ref[...])
    for i in range(NEAR):
        out_ref[i] = rows


def last_kernel(recv_ref, run_ref, sums_ref, all_ref):
    def base_row(row):
        row += ROUNDS * NEAR
        return jnp.concatenate([recv_ref[b, row : row + 1] for b in range(NEAR)], axis=0)

    rows_norm = base_row(0)
    running = base_row(1)
    lane = iota((NC * FAR, 128), 1)
    sums = jnp.where(lane == 0, jnp.sum(running), 0.0)
    for r in range(ROUNDS):
        least = recv_ref[0, r * NEAR : (r + 1) * NEAR]
        for s in range(1, NEAR):
            least = jnp.minimum(least, recv_ref[s, r * NEAR : (r + 1) * NEAR])
        running = jnp.minimum(running, jnp.maximum(rows_norm + least, 0.0))
        sums = jnp.where(lane == r + 1, jnp.sum(running), sums)
    for b in range(NEAR):
        all_ref[b] = running[b : b + 1]
    run_ref[...] = all_ref[lax.axis_index("x")]
    sums_ref[...] = sums


def relay_kernel(recv_ref, out_ref):
    total = jnp.sum(recv_ref[...], axis=0, keepdims=True)
    out_ref[...] = jnp.broadcast_to(total, (NZ, 128))


def final_kernel(recv_ref, run_ref, dist_ref, weight_ref, pot_ref):
    total = jnp.sum(recv_ref[...], axis=0, keepdims=True)
    lane = iota((1, 128), 1)
    last = jnp.sum(jnp.where(lane == ROUNDS, total, 0.0), axis=1, keepdims=True)
    running = run_ref[...]
    dist_ref[...] = running.reshape(ROWS_DEV)
    weight_ref[...] = (running * (ROWS / last)).reshape(ROWS_DEV)
    pot_ref[...] = total.reshape(128)[0 : ROUNDS + 1]


def vspec():
    return pl.BlockSpec(memory_space=VMEM)


def call(kernel, ins, outs, scratch=(), near=True):
    shapes = [VMEM(s, d) if near else jax.ShapeDtypeStruct(s, d) for s, d in outs]
    single = len(shapes) == 1
    kern = pl.pallas_call(
        kernel,
        in_specs=ins,
        out_specs=vspec() if single else [vspec() for _ in shapes],
        out_shape=shapes[0] if single else shapes,
        scratch_shapes=list(scratch),
        compiler_params=pltpu.CompilerParams(vmem_limit_bytes=16 << 20),
    )

    def run(*args):
        placed = []
        for a, i in zip(args, ins):
            space = VMEM if i.memory_space == VMEM else pltpu.HBM
            placed.append(pltpu.with_memory_space_constraint(a, space))
        return kern(*placed)

    return run


def body(points, first_center, counts, cand_index):
    pack = call(
        pack_kernel,
        [pl.BlockSpec(memory_space=pl.ANY)] * 3,
        [((PLANE, ROUNDS, CAP, D), BF16)],
        [
            SMEM((ROUNDS,), jnp.int32),
            SMEM((ROUNDS, 1, 1, CAP), jnp.int32),
            VMEM((ROWS_DEV, D), BF16),
            pltpu.SemaphoreType.DMA((3,)),
        ],
    )
    blocks = pack(counts.reshape(ROUNDS), cand_index, points)
    plane = ("y", "x")
    blocks, early = lax.optimization_barrier((blocks, points))
    blocks = lax.all_to_all(blocks, plane, 0, 0)
    compact = call(
        compact_kernel,
        [vspec()],
        [((NZ, ROUNDS * FOLD, LANES), BF16)],
        [VMEM((PLANE * SLOTS, D), F32), VMEM((ROUNDS * FOLD, LANES), F32)],
    )
    mine = compact(blocks)
    mine = lax.all_to_all(mine, "z", 0, 0)

    def from_side(rows, k):
        return lax.ppermute(rows, "x", [((i + k) % NX, i) for i in range(NX)])

    right = from_side(early, 1)
    far_side = lax.ppermute(right, "x", [((i + 1) % NX, i) for i in range(NX)])
    line = [points, right, far_side, from_side(early, 3)]
    base = call(base_kernel, [vspec()] * 2, [((2, ROWS_DEV), F32)])(points, first_center)
    spread = call(spread_kernel, [vspec()], [((FAR, KEEP, D), BF16)])
    mine = mine.reshape(NZ * ROUNDS * FOLD, LANES)
    cands = lax.all_to_all(spread(mine), "y", 0, 0).reshape(FAR * KEEP, D)
    others = lax.ppermute(cands, "c", [(0, 1), (1, 0)])
    rows = ((4 * NEAR, ROWS_DEV), F32)
    own = call(own_kernel, [vspec()] * (2 + NEAR), [rows])
    other = call(other_kernel, [vspec()] * (2 + NEAR), [((NEAR, *rows[0]), F32)], [VMEM(*rows)])
    mins = lax.all_to_all(other(own(base, cands, *line), others, *line), "x", 0, 0)
    last = call(
        last_kernel,
        [vspec()],
        [((1, ROWS_DEV), F32), ((NC * FAR, 128), F32)],
        [VMEM((NEAR, 1, ROWS_DEV), F32)],
    )
    running, sums = last(mins)
    sums = lax.all_to_all(sums, ("c", "y"), 0, 0)
    relay = call(relay_kernel, [vspec()], [((NZ, 128), F32)])
    sums = lax.all_to_all(relay(sums), "z", 0, 0)
    final = call(
        final_kernel,
        [vspec()] * 2,
        [((ROWS_DEV,), F32), ((ROWS_DEV,), F32), ((ROUNDS + 1,), F32)],
        near=False,
    )
    return tuple(final(sums, running))


def solution(mesh):
    axes = ("z", "c", "y", "x")
    grid = Mesh(mesh.devices.reshape(NZ, NC, NY, NX), axes)
    placed = (P(axes, None), P(), P(None, ("z", "c"), ("y", "x")), P(None, ("z", "c"), ("y", "x"), None))

    return jax.shard_map(
        body,
        mesh=grid,
        in_specs=placed,
        out_specs=(P(axes), P(axes), P()),
        check_vma=False,
    )
```

```python
import jax
import jax.numpy as jnp
from jax import lax
from jax.experimental import pallas as pl
from jax.experimental.pallas import tpu as pltpu
from jax.sharding import Mesh
from jax.sharding import PartitionSpec as P


D = 1024
ROWS_DEV = 256
ROUNDS = 3
CAP = 4
ROWS = 131072
NZ, NC, NY, NX = 16, 2, 4, 4
PLANE = NY * NX
FAR = NY
NEAR = NX
SLOTS = ROUNDS * CAP
LANES = 128
Z_GROUP = [[(i + NZ // 2) % NZ for i in range(NZ)]]
FOLD = D // LANES
KEEP = ROUNDS * NZ

VMEM = pltpu.VMEM
SMEM = pltpu.SMEM
F32 = jnp.float32
BF16 = jnp.bfloat16


def iota(shape, dim):
    return lax.broadcasted_iota(jnp.int32, shape, dim)


def one_hot(cond):
    return jnp.where(cond, 1.0, 0.0).astype(BF16)


def dot_nt(a, b):
    return lax.dot_general(a, b, (((1,), (1,)), ((), ())), preferred_element_type=F32)


def pack_kernel(cnt_hbm, idx_hbm, pts_hbm, out_ref, cnt_ref, idx_ref, pts_ref, sem):
    fetch_idx = pltpu.make_async_copy(idx_hbm, idx_ref, sem.at[0])
    fetch_cnt = pltpu.make_async_copy(cnt_hbm, cnt_ref, sem.at[1])
    fetch = pltpu.make_async_copy(pts_hbm, pts_ref, sem.at[2])
    fetch_idx.start()
    fetch_cnt.start()
    fetch.start()
    fetch_idx.wait()
    fetch_cnt.wait()
    sub = iota((16, ROWS_DEV), 0)
    lane = iota((16, ROWS_DEV), 1)
    want = jnp.full((16, ROWS_DEV), -1, jnp.int32)
    for q in range(SLOTS):
        r, j = divmod(q, CAP)
        row = jnp.where(j < cnt_ref[r], idx_ref[r, 0, 0, j], -1)
        want = jnp.where(sub == q, row, want)
    fetch.wait()
    rows = jnp.dot(one_hot(lane == want), pts_ref[...], preferred_element_type=F32)
    dead = jnp.logical_and(want < 0, lane == 0)[:, :LANES]
    head = jnp.where(dead, jnp.inf, rows[:, :LANES]).astype(BF16)
    tail = rows[:, LANES:].astype(BF16)
    for i in range(PLANE):
        for r in range(ROUNDS):
            out_ref[i, r, :, :LANES] = head[r * CAP : (r + 1) * CAP]
            out_ref[i, r, :, LANES:] = tail[r * CAP : (r + 1) * CAP]


def compact_kernel(recv_ref, out_ref, tmp_ref, fold_ref):
    place = lax.axis_index("y") * NX + lax.axis_index("x")
    n = PLANE * SLOTS
    for s in range(PLANE):
        for r in range(ROUNDS):
            at = s * SLOTS + r * CAP
            tmp_ref[at : at + CAP, :] = recv_ref[s, r].astype(F32)
    head = tmp_ref[:, :LANES]
    dead = head == jnp.inf
    live = one_hot(jnp.logical_not(dead))
    src = iota((n, n), 0)
    dst = iota((n, n), 1)
    same = src % SLOTS // CAP == dst % SLOTS // CAP
    before = one_hot(jnp.logical_and(same, src < dst))
    here = one_hot(src == dst)
    contract = (((0,), (0,)), ((), ()))
    pos = lax.dot_general(live, before, contract, preferred_element_type=F32)[0:1]
    alive = lax.dot_general(live, here, contract, preferred_element_type=F32)[0:1]
    slot = jnp.where(alive > 0.5, pos, -1.0)
    round_of = iota((16, n), 1) % SLOTS // CAP
    take = jnp.logical_and(round_of == iota((16, n), 0), slot == place.astype(F32))
    take = one_hot(take)
    head = jnp.where(dead, 0.0, head).astype(BF16)
    head = jnp.dot(take, head, preferred_element_type=F32)
    tail = jnp.dot(take, tmp_ref[:, LANES:].astype(BF16), preferred_element_type=F32)
    rows = jnp.concatenate([head, tail], axis=1)
    for r in range(ROUNDS):
        for f in range(FOLD):
            at = r * FOLD + f
            fold_ref[at : at + 1, :] = rows[r : r + 1, f * LANES : (f + 1) * LANES]
    block = fold_ref[...].astype(BF16)
    for i in range(NZ):
        out_ref[i] = block


def spread_kernel(recv_ref, out_ref):
    n = NZ * ROUNDS * FOLD
    m = iota((n, n), 0)
    k = iota((n, n), 1)
    z = m % NZ
    r = m // NZ % ROUNDS
    f = m // KEEP
    sel = one_hot(k == (z * ROUNDS + r) * FOLD + f)
    parts = jnp.dot(sel, recv_ref[...], preferred_element_type=F32).astype(BF16)
    for i in range(FAR):
        for f in range(FOLD):
            out_ref[i, :, f * LANES : (f + 1) * LANES] = parts[f * KEEP : (f + 1) * KEEP]


def base_kernel(pts_ref, center_ref, out_ref):
    pts = pts_ref[...]
    wide = pts.astype(F32)
    sq = wide * wide
    hi = sq.astype(BF16)
    lo = (sq - hi.astype(F32)).astype(BF16)
    ones = jnp.ones((16, D), BF16)
    rows_norm = (dot_nt(ones, hi) + dot_nt(ones, lo))[0:1]
    center = jnp.broadcast_to(center_ref[...].reshape(1, D), (16, D))
    cwide = center.astype(F32)
    cnorm = jnp.sum(cwide * cwide, axis=1, keepdims=True)
    first = (cnorm - 2.0 * dot_nt(center, pts))[0:1]
    out_ref[0:1] = rows_norm
    out_ref[1:2] = jnp.maximum(rows_norm + first, 0.0)


def line_mins(cands_ref, pts_refs, rows_ref):
    cands = cands_ref[...]
    wide = cands.astype(F32)
    norm = jnp.sum(wide * wide, axis=1, keepdims=True)
    place = lax.axis_index("x")
    for k, pts_ref in enumerate(pts_refs):
        block = (place + k) % NEAR
        val = (norm - 2.0 * dot_nt(cands, pts_ref[...])).reshape(FAR, ROUNDS, NZ, ROWS_DEV)
        least = jnp.min(jnp.min(val, axis=0), axis=1)
        for r in range(ROUNDS):
            rows_ref[pl.ds(r * NEAR + block, 1), :] = least[r : r + 1]


def own_kernel(base_ref, cands_ref, *refs):
    *pts_refs, rows_ref = refs
    rows_ref[ROUNDS * NEAR : ROUNDS * NEAR + 2, :] = base_ref[...]
    rows_ref[ROUNDS * NEAR + 2 :, :] = jnp.zeros((NEAR - 2, ROWS_DEV), F32)
    line_mins(cands_ref, pts_refs, rows_ref)


def other_kernel(own_ref, cands_ref, *refs):
    *pts_refs, out_ref, rows_ref = refs
    rows_ref[...] = own_ref[...]
    line_mins(cands_ref, pts_refs, rows_ref)
    rows = jnp.minimum(rows_ref[...], own_ref[...])
    for i in range(NEAR):
        out_ref[i] = rows


def last_kernel(recv_ref, run_ref, sums_ref, all_ref):
    def base_row(row):
        row += ROUNDS * NEAR
        return jnp.concatenate([recv_ref[b, row : row + 1] for b in range(NEAR)], axis=0)

    rows_norm = base_row(0)
    running = base_row(1)
    lane = iota((NC * FAR, 128), 1)
    sums = jnp.where(lane == 0, jnp.sum(running), 0.0)
    for r in range(ROUNDS):
        least = recv_ref[0, r * NEAR : (r + 1) * NEAR]
        for s in range(1, NEAR):
            least = jnp.minimum(least, recv_ref[s, r * NEAR : (r + 1) * NEAR])
        running = jnp.minimum(running, jnp.maximum(rows_norm + least, 0.0))
        sums = jnp.where(lane == r + 1, jnp.sum(running), sums)
    for b in range(NEAR):
        all_ref[b] = running[b : b + 1]
    run_ref[...] = all_ref[lax.axis_index("x")]
    sums_ref[...] = sums


def relay_kernel(recv_ref, out_ref):
    total = jnp.sum(recv_ref[...], axis=0, keepdims=True)
    out_ref[...] = jnp.broadcast_to(total, (NZ, 128))


def final_kernel(recv_ref, run_ref, dist_ref, weight_ref, pot_ref):
    total = jnp.sum(recv_ref[...], axis=0, keepdims=True)
    lane = iota((1, 128), 1)
    last = jnp.sum(jnp.where(lane == ROUNDS, total, 0.0), axis=1, keepdims=True)
    running = run_ref[...]
    dist_ref[...] = running.reshape(ROWS_DEV)
    weight_ref[...] = (running * (ROWS / last)).reshape(ROWS_DEV)
    pot_ref[...] = total.reshape(128)[0 : ROUNDS + 1]


def vspec():
    return pl.BlockSpec(memory_space=VMEM)


def call(kernel, ins, outs, scratch=(), near=True):
    shapes = [VMEM(s, d) if near else jax.ShapeDtypeStruct(s, d) for s, d in outs]
    single = len(shapes) == 1
    kern = pl.pallas_call(
        kernel,
        in_specs=ins,
        out_specs=vspec() if single else [vspec() for _ in shapes],
        out_shape=shapes[0] if single else shapes,
        scratch_shapes=list(scratch),
        compiler_params=pltpu.CompilerParams(vmem_limit_bytes=16 << 20),
    )

    def run(*args):
        placed = []
        for a, i in zip(args, ins):
            space = VMEM if i.memory_space == VMEM else pltpu.HBM
            placed.append(pltpu.with_memory_space_constraint(a, space))
        return kern(*placed)

    return run


def body(points, first_center, counts, cand_index):
    pack = call(
        pack_kernel,
        [pl.BlockSpec(memory_space=pl.ANY)] * 3,
        [((PLANE, ROUNDS, CAP, D), BF16)],
        [
            SMEM((ROUNDS,), jnp.int32),
            SMEM((ROUNDS, 1, 1, CAP), jnp.int32),
            VMEM((ROWS_DEV, D), BF16),
            pltpu.SemaphoreType.DMA((3,)),
        ],
    )
    blocks = pack(counts.reshape(ROUNDS), cand_index, points)
    plane = ("y", "x")
    blocks, early = lax.optimization_barrier((blocks, points))
    blocks = lax.all_to_all(blocks, plane, 0, 0)
    compact = call(
        compact_kernel,
        [vspec()],
        [((NZ, ROUNDS * FOLD, LANES), BF16)],
        [VMEM((PLANE * SLOTS, D), F32), VMEM((ROUNDS * FOLD, LANES), F32)],
    )
    mine = compact(blocks)
    mine = lax.all_to_all(mine, "z", 0, 0, axis_index_groups=Z_GROUP)

    def from_side(rows, k):
        return lax.ppermute(rows, "x", [((i + k) % NX, i) for i in range(NX)])

    right = from_side(early, 1)
    far_side = lax.ppermute(right, "x", [((i + 1) % NX, i) for i in range(NX)])
    line = [points, right, far_side, from_side(early, 3)]
    base = call(base_kernel, [vspec()] * 2, [((2, ROWS_DEV), F32)])(points, first_center)
    spread = call(spread_kernel, [vspec()], [((FAR, KEEP, D), BF16)])
    mine = mine.reshape(NZ * ROUNDS * FOLD, LANES)
    cands = lax.all_to_all(spread(mine), "y", 0, 0).reshape(FAR * KEEP, D)
    others = lax.ppermute(cands, "c", [(0, 1), (1, 0)])
    rows = ((4 * NEAR, ROWS_DEV), F32)
    own = call(own_kernel, [vspec()] * (2 + NEAR), [rows])
    other = call(other_kernel, [vspec()] * (2 + NEAR), [((NEAR, *rows[0]), F32)], [VMEM(*rows)])
    mins = lax.all_to_all(other(own(base, cands, *line), others, *line), "x", 0, 0)
    last = call(
        last_kernel,
        [vspec()],
        [((1, ROWS_DEV), F32), ((NC * FAR, 128), F32)],
        [VMEM((NEAR, 1, ROWS_DEV), F32)],
    )
    running, sums = last(mins)
    sums = lax.all_to_all(sums, ("c", "y"), 0, 0)
    relay = call(relay_kernel, [vspec()], [((NZ, 128), F32)])
    sums = lax.all_to_all(relay(sums), "z", 0, 0, axis_index_groups=Z_GROUP)
    final = call(
        final_kernel,
        [vspec()] * 2,
        [((ROWS_DEV,), F32), ((ROWS_DEV,), F32), ((ROUNDS + 1,), F32)],
        near=False,
    )
    return tuple(final(sums, running))


def solution(mesh):
    axes = ("z", "c", "y", "x")
    grid = Mesh(mesh.devices.reshape(NZ, NC, NY, NX), axes)
    placed = (P(axes, None), P(), P(None, ("z", "c"), ("y", "x")), P(None, ("z", "c"), ("y", "x"), None))

    return jax.shard_map(
        body,
        mesh=grid,
        in_specs=placed,
        out_specs=(P(axes), P(axes), P()),
        check_vma=False,
    )
```

```python
import jax
import jax.numpy as jnp
from jax import lax
from jax.experimental import pallas as pl
from jax.experimental.pallas import tpu as pltpu
from jax.sharding import Mesh
from jax.sharding import PartitionSpec as P


D = 1024
ROWS_DEV = 256
ROUNDS = 3
CAP = 4
ROWS = 131072
NZ, NC, NY, NX = 16, 2, 4, 4
PLANE = NY * NX
FAR = NY
NEAR = NX
SLOTS = ROUNDS * CAP
LANES = 128


def led_by(size, first):
    return [[(first + i) % size for i in range(size)]]


Z_GROUP = led_by(NZ, 9)
PLANE_GROUP = led_by(PLANE, 15)
Y_GROUP = led_by(NY, 2)
X_FIRST = 2
X_GROUP = led_by(NX, X_FIRST)
CORE_Y_GROUP = led_by(NC * NY, 6)
FOLD = D // LANES
KEEP = ROUNDS * NZ

VMEM = pltpu.VMEM
SMEM = pltpu.SMEM
F32 = jnp.float32
BF16 = jnp.bfloat16


def iota(shape, dim):
    return lax.broadcasted_iota(jnp.int32, shape, dim)


def one_hot(cond):
    return jnp.where(cond, 1.0, 0.0).astype(BF16)


def dot_nt(a, b):
    return lax.dot_general(a, b, (((1,), (1,)), ((), ())), preferred_element_type=F32)


def pack_kernel(cnt_hbm, idx_hbm, pts_hbm, out_ref, cnt_ref, idx_ref, pts_ref, sem):
    fetch_idx = pltpu.make_async_copy(idx_hbm, idx_ref, sem.at[0])
    fetch_cnt = pltpu.make_async_copy(cnt_hbm, cnt_ref, sem.at[1])
    fetch = pltpu.make_async_copy(pts_hbm, pts_ref, sem.at[2])
    fetch_idx.start()
    fetch_cnt.start()
    fetch.start()
    fetch_idx.wait()
    fetch_cnt.wait()
    sub = iota((16, ROWS_DEV), 0)
    lane = iota((16, ROWS_DEV), 1)
    want = jnp.full((16, ROWS_DEV), -1, jnp.int32)
    for q in range(SLOTS):
        r, j = divmod(q, CAP)
        row = jnp.where(j < cnt_ref[r], idx_ref[r, 0, 0, j], -1)
        want = jnp.where(sub == q, row, want)
    fetch.wait()
    rows = jnp.dot(one_hot(lane == want), pts_ref[...], preferred_element_type=F32)
    dead = jnp.logical_and(want < 0, lane == 0)[:, :LANES]
    head = jnp.where(dead, jnp.inf, rows[:, :LANES]).astype(BF16)
    tail = rows[:, LANES:].astype(BF16)
    for i in range(PLANE):
        for r in range(ROUNDS):
            out_ref[i, r, :, :LANES] = head[r * CAP : (r + 1) * CAP]
            out_ref[i, r, :, LANES:] = tail[r * CAP : (r + 1) * CAP]


def compact_kernel(recv_ref, out_ref, tmp_ref, fold_ref):
    place = lax.axis_index("y") * NX + lax.axis_index("x")
    n = PLANE * SLOTS
    for s in range(PLANE):
        for r in range(ROUNDS):
            at = s * SLOTS + r * CAP
            tmp_ref[at : at + CAP, :] = recv_ref[s, r].astype(F32)
    head = tmp_ref[:, :LANES]
    dead = head == jnp.inf
    live = one_hot(jnp.logical_not(dead))
    src = iota((n, n), 0)
    dst = iota((n, n), 1)
    same = src % SLOTS // CAP == dst % SLOTS // CAP
    before = one_hot(jnp.logical_and(same, src < dst))
    here = one_hot(src == dst)
    contract = (((0,), (0,)), ((), ()))
    pos = lax.dot_general(live, before, contract, preferred_element_type=F32)[0:1]
    alive = lax.dot_general(live, here, contract, preferred_element_type=F32)[0:1]
    slot = jnp.where(alive > 0.5, pos, -1.0)
    round_of = iota((16, n), 1) % SLOTS // CAP
    take = jnp.logical_and(round_of == iota((16, n), 0), slot == place.astype(F32))
    take = one_hot(take)
    head = jnp.where(dead, 0.0, head).astype(BF16)
    head = jnp.dot(take, head, preferred_element_type=F32)
    tail = jnp.dot(take, tmp_ref[:, LANES:].astype(BF16), preferred_element_type=F32)
    rows = jnp.concatenate([head, tail], axis=1)
    for r in range(ROUNDS):
        for f in range(FOLD):
            at = r * FOLD + f
            fold_ref[at : at + 1, :] = rows[r : r + 1, f * LANES : (f + 1) * LANES]
    block = fold_ref[...].astype(BF16)
    for i in range(NZ):
        out_ref[i] = block


def spread_kernel(recv_ref, out_ref):
    n = NZ * ROUNDS * FOLD
    m = iota((n, n), 0)
    k = iota((n, n), 1)
    z = m % NZ
    r = m // NZ % ROUNDS
    f = m // KEEP
    sel = one_hot(k == (z * ROUNDS + r) * FOLD + f)
    parts = jnp.dot(sel, recv_ref[...], preferred_element_type=F32).astype(BF16)
    for i in range(FAR):
        for f in range(FOLD):
            out_ref[i, :, f * LANES : (f + 1) * LANES] = parts[f * KEEP : (f + 1) * KEEP]


def base_kernel(pts_ref, center_ref, out_ref):
    pts = pts_ref[...]
    wide = pts.astype(F32)
    sq = wide * wide
    hi = sq.astype(BF16)
    lo = (sq - hi.astype(F32)).astype(BF16)
    ones = jnp.ones((16, D), BF16)
    rows_norm = (dot_nt(ones, hi) + dot_nt(ones, lo))[0:1]
    center = jnp.broadcast_to(center_ref[...].reshape(1, D), (16, D))
    cwide = center.astype(F32)
    cnorm = jnp.sum(cwide * cwide, axis=1, keepdims=True)
    first = (cnorm - 2.0 * dot_nt(center, pts))[0:1]
    out_ref[0:1] = rows_norm
    out_ref[1:2] = jnp.maximum(rows_norm + first, 0.0)


def line_mins(cands_ref, pts_refs, rows_ref):
    cands = cands_ref[...]
    wide = cands.astype(F32)
    norm = jnp.sum(wide * wide, axis=1, keepdims=True)
    place = lax.axis_index("x")
    for k, pts_ref in enumerate(pts_refs):
        block = (place + k) % NEAR
        val = (norm - 2.0 * dot_nt(cands, pts_ref[...])).reshape(FAR, ROUNDS, NZ, ROWS_DEV)
        least = jnp.min(jnp.min(val, axis=0), axis=1)
        for r in range(ROUNDS):
            rows_ref[pl.ds(r * NEAR + block, 1), :] = least[r : r + 1]


def own_kernel(base_ref, cands_ref, *refs):
    *pts_refs, rows_ref = refs
    rows_ref[ROUNDS * NEAR : ROUNDS * NEAR + 2, :] = base_ref[...]
    rows_ref[ROUNDS * NEAR + 2 :, :] = jnp.zeros((NEAR - 2, ROWS_DEV), F32)
    line_mins(cands_ref, pts_refs, rows_ref)


def other_kernel(own_ref, cands_ref, *refs):
    *pts_refs, out_ref, rows_ref = refs
    rows_ref[...] = own_ref[...]
    line_mins(cands_ref, pts_refs, rows_ref)
    rows = jnp.minimum(rows_ref[...], own_ref[...])
    for i in range(NEAR):
        out_ref[i] = rows


def last_kernel(recv_ref, run_ref, sums_ref, all_ref):
    def base_row(row):
        row += ROUNDS * NEAR
        return jnp.concatenate([recv_ref[(b - X_FIRST) % NEAR, row : row + 1] for b in range(NEAR)], axis=0)

    rows_norm = base_row(0)
    running = base_row(1)
    lane = iota((NC * FAR, 128), 1)
    sums = jnp.where(lane == 0, jnp.sum(running), 0.0)
    for r in range(ROUNDS):
        least = recv_ref[0, r * NEAR : (r + 1) * NEAR]
        for s in range(1, NEAR):
            least = jnp.minimum(least, recv_ref[s, r * NEAR : (r + 1) * NEAR])
        running = jnp.minimum(running, jnp.maximum(rows_norm + least, 0.0))
        sums = jnp.where(lane == r + 1, jnp.sum(running), sums)
    for b in range(NEAR):
        all_ref[b] = running[b : b + 1]
    run_ref[...] = all_ref[lax.axis_index("x")]
    sums_ref[...] = sums


def relay_kernel(recv_ref, out_ref):
    total = jnp.sum(recv_ref[...], axis=0, keepdims=True)
    out_ref[...] = jnp.broadcast_to(total, (NZ, 128))


def final_kernel(recv_ref, run_ref, dist_ref, weight_ref, pot_ref):
    total = jnp.sum(recv_ref[...], axis=0, keepdims=True)
    lane = iota((1, 128), 1)
    last = jnp.sum(jnp.where(lane == ROUNDS, total, 0.0), axis=1, keepdims=True)
    running = run_ref[...]
    dist_ref[...] = running.reshape(ROWS_DEV)
    weight_ref[...] = (running * (ROWS / last)).reshape(ROWS_DEV)
    pot_ref[...] = total.reshape(128)[0 : ROUNDS + 1]


def vspec():
    return pl.BlockSpec(memory_space=VMEM)


def call(kernel, ins, outs, scratch=(), near=True):
    shapes = [VMEM(s, d) if near else jax.ShapeDtypeStruct(s, d) for s, d in outs]
    single = len(shapes) == 1
    kern = pl.pallas_call(
        kernel,
        in_specs=ins,
        out_specs=vspec() if single else [vspec() for _ in shapes],
        out_shape=shapes[0] if single else shapes,
        scratch_shapes=list(scratch),
        compiler_params=pltpu.CompilerParams(vmem_limit_bytes=16 << 20),
    )

    def run(*args):
        placed = []
        for a, i in zip(args, ins):
            space = VMEM if i.memory_space == VMEM else pltpu.HBM
            placed.append(pltpu.with_memory_space_constraint(a, space))
        return kern(*placed)

    return run


def body(points, first_center, counts, cand_index):
    pack = call(
        pack_kernel,
        [pl.BlockSpec(memory_space=pl.ANY)] * 3,
        [((PLANE, ROUNDS, CAP, D), BF16)],
        [
            SMEM((ROUNDS,), jnp.int32),
            SMEM((ROUNDS, 1, 1, CAP), jnp.int32),
            VMEM((ROWS_DEV, D), BF16),
            pltpu.SemaphoreType.DMA((3,)),
        ],
    )
    blocks = pack(counts.reshape(ROUNDS), cand_index, points)
    plane = ("y", "x")
    blocks, early = lax.optimization_barrier((blocks, points))
    blocks = lax.all_to_all(blocks, plane, 0, 0, axis_index_groups=PLANE_GROUP)
    compact = call(
        compact_kernel,
        [vspec()],
        [((NZ, ROUNDS * FOLD, LANES), BF16)],
        [VMEM((PLANE * SLOTS, D), F32), VMEM((ROUNDS * FOLD, LANES), F32)],
    )
    mine = compact(blocks)
    mine = lax.all_to_all(mine, "z", 0, 0, axis_index_groups=Z_GROUP)

    def from_side(rows, k):
        return lax.ppermute(rows, "x", [((i + k) % NX, i) for i in range(NX)])

    right = from_side(early, 1)
    far_side = lax.ppermute(right, "x", [((i + 1) % NX, i) for i in range(NX)])
    line = [points, right, far_side, from_side(early, 3)]
    base = call(base_kernel, [vspec()] * 2, [((2, ROWS_DEV), F32)])(points, first_center)
    spread = call(spread_kernel, [vspec()], [((FAR, KEEP, D), BF16)])
    mine = mine.reshape(NZ * ROUNDS * FOLD, LANES)
    cands = lax.all_to_all(spread(mine), "y", 0, 0, axis_index_groups=Y_GROUP).reshape(FAR * KEEP, D)
    others = lax.ppermute(cands, "c", [(0, 1), (1, 0)])
    rows = ((4 * NEAR, ROWS_DEV), F32)
    own = call(own_kernel, [vspec()] * (2 + NEAR), [rows])
    other = call(other_kernel, [vspec()] * (2 + NEAR), [((NEAR, *rows[0]), F32)], [VMEM(*rows)])
    mins = other(own(base, cands, *line), others, *line)
    mins = lax.all_to_all(mins, "x", 0, 0, axis_index_groups=X_GROUP)
    last = call(
        last_kernel,
        [vspec()],
        [((1, ROWS_DEV), F32), ((NC * FAR, 128), F32)],
        [VMEM((NEAR, 1, ROWS_DEV), F32)],
    )
    running, sums = last(mins)
    sums = lax.all_to_all(sums, ("c", "y"), 0, 0, axis_index_groups=CORE_Y_GROUP)
    relay = call(relay_kernel, [vspec()], [((NZ, 128), F32)])
    sums = lax.all_to_all(relay(sums), "z", 0, 0, axis_index_groups=Z_GROUP)
    final = call(
        final_kernel,
        [vspec()] * 2,
        [((ROWS_DEV,), F32), ((ROWS_DEV,), F32), ((ROUNDS + 1,), F32)],
        near=False,
    )
    return tuple(final(sums, running))


def solution(mesh):
    axes = ("z", "c", "y", "x")
    grid = Mesh(mesh.devices.reshape(NZ, NC, NY, NX), axes)
    placed = (P(axes, None), P(), P(None, ("z", "c"), ("y", "x")), P(None, ("z", "c"), ("y", "x"), None))

    return jax.shard_map(
        body,
        mesh=grid,
        in_specs=placed,
        out_specs=(P(axes), P(axes), P()),
        check_vma=False,
    )
```

```python
import jax
import jax.numpy as jnp
from jax import lax
from jax.experimental import pallas as pl
from jax.experimental.pallas import tpu as pltpu
from jax.sharding import Mesh
from jax.sharding import PartitionSpec as P


D = 1024
ROWS_DEV = 256
ROUNDS = 3
CAP = 4
ROWS = 131072
NZ, NC, NY, NX = 16, 2, 4, 4
PLANE = NY * NX
FAR = NY
NEAR = NX
SLOTS = ROUNDS * CAP
LANES = 128


def led_by(size, first):
    return [[(first + i) % size for i in range(size)]]


Z_GROUP = led_by(NZ, 10)
PLANE_GROUP = led_by(PLANE, 15)
Y_GROUP = led_by(NY, 2)
X_FIRST = 2
X_GROUP = led_by(NX, X_FIRST)
SUM_GROUP = led_by(NZ * NC * NY, 86)
FOLD = D // LANES
KEEP = ROUNDS * NZ

VMEM = pltpu.VMEM
SMEM = pltpu.SMEM
F32 = jnp.float32
BF16 = jnp.bfloat16


def iota(shape, dim):
    return lax.broadcasted_iota(jnp.int32, shape, dim)


def one_hot(cond):
    return jnp.where(cond, 1.0, 0.0).astype(BF16)


def dot_nt(a, b):
    return lax.dot_general(a, b, (((1,), (1,)), ((), ())), preferred_element_type=F32)


def pack_kernel(cnt_hbm, idx_hbm, pts_hbm, out_ref, cnt_ref, idx_ref, pts_ref, sem):
    fetch_idx = pltpu.make_async_copy(idx_hbm, idx_ref, sem.at[0])
    fetch_cnt = pltpu.make_async_copy(cnt_hbm, cnt_ref, sem.at[1])
    fetch = pltpu.make_async_copy(pts_hbm, pts_ref, sem.at[2])
    fetch_idx.start()
    fetch_cnt.start()
    fetch.start()
    fetch_idx.wait()
    fetch_cnt.wait()
    sub = iota((16, ROWS_DEV), 0)
    lane = iota((16, ROWS_DEV), 1)
    want = jnp.full((16, ROWS_DEV), -1, jnp.int32)
    for q in range(SLOTS):
        r, j = divmod(q, CAP)
        row = jnp.where(j < cnt_ref[r], idx_ref[r, 0, 0, j], -1)
        want = jnp.where(sub == q, row, want)
    fetch.wait()
    rows = jnp.dot(one_hot(lane == want), pts_ref[...], preferred_element_type=F32)
    dead = jnp.logical_and(want < 0, lane == 0)[:, :LANES]
    head = jnp.where(dead, jnp.inf, rows[:, :LANES]).astype(BF16)
    tail = rows[:, LANES:].astype(BF16)
    for i in range(PLANE):
        for r in range(ROUNDS):
            out_ref[i, r, :, :LANES] = head[r * CAP : (r + 1) * CAP]
            out_ref[i, r, :, LANES:] = tail[r * CAP : (r + 1) * CAP]


def compact_kernel(recv_ref, out_ref, tmp_ref, fold_ref):
    place = lax.axis_index("y") * NX + lax.axis_index("x")
    n = PLANE * SLOTS
    for s in range(PLANE):
        for r in range(ROUNDS):
            at = s * SLOTS + r * CAP
            tmp_ref[at : at + CAP, :] = recv_ref[s, r].astype(F32)
    head = tmp_ref[:, :LANES]
    dead = head == jnp.inf
    live = one_hot(jnp.logical_not(dead))
    src = iota((n, n), 0)
    dst = iota((n, n), 1)
    same = src % SLOTS // CAP == dst % SLOTS // CAP
    before = one_hot(jnp.logical_and(same, src < dst))
    here = one_hot(src == dst)
    contract = (((0,), (0,)), ((), ()))
    pos = lax.dot_general(live, before, contract, preferred_element_type=F32)[0:1]
    alive = lax.dot_general(live, here, contract, preferred_element_type=F32)[0:1]
    slot = jnp.where(alive > 0.5, pos, -1.0)
    round_of = iota((16, n), 1) % SLOTS // CAP
    take = jnp.logical_and(round_of == iota((16, n), 0), slot == place.astype(F32))
    take = one_hot(take)
    head = jnp.where(dead, 0.0, head).astype(BF16)
    head = jnp.dot(take, head, preferred_element_type=F32)
    tail = jnp.dot(take, tmp_ref[:, LANES:].astype(BF16), preferred_element_type=F32)
    rows = jnp.concatenate([head, tail], axis=1)
    for r in range(ROUNDS):
        for f in range(FOLD):
            at = r * FOLD + f
            fold_ref[at : at + 1, :] = rows[r : r + 1, f * LANES : (f + 1) * LANES]
    block = fold_ref[...].astype(BF16)
    for i in range(NZ):
        out_ref[i] = block


def spread_kernel(recv_ref, out_ref):
    n = NZ * ROUNDS * FOLD
    m = iota((n, n), 0)
    k = iota((n, n), 1)
    z = m % NZ
    r = m // NZ % ROUNDS
    f = m // KEEP
    sel = one_hot(k == (z * ROUNDS + r) * FOLD + f)
    parts = jnp.dot(sel, recv_ref[...], preferred_element_type=F32).astype(BF16)
    for i in range(FAR):
        for f in range(FOLD):
            out_ref[i, :, f * LANES : (f + 1) * LANES] = parts[f * KEEP : (f + 1) * KEEP]


def base_kernel(pts_ref, center_ref, out_ref):
    pts = pts_ref[...]
    wide = pts.astype(F32)
    sq = wide * wide
    hi = sq.astype(BF16)
    lo = (sq - hi.astype(F32)).astype(BF16)
    ones = jnp.ones((16, D), BF16)
    rows_norm = (dot_nt(ones, hi) + dot_nt(ones, lo))[0:1]
    center = jnp.broadcast_to(center_ref[...].reshape(1, D), (16, D))
    cwide = center.astype(F32)
    cnorm = jnp.sum(cwide * cwide, axis=1, keepdims=True)
    first = (cnorm - 2.0 * dot_nt(center, pts))[0:1]
    out_ref[0:1] = rows_norm
    out_ref[1:2] = jnp.maximum(rows_norm + first, 0.0)


def line_mins(cands_ref, pts_refs, rows_ref):
    cands = cands_ref[...]
    wide = cands.astype(F32)
    norm = jnp.sum(wide * wide, axis=1, keepdims=True)
    place = lax.axis_index("x")
    for k, pts_ref in enumerate(pts_refs):
        block = (place + k) % NEAR
        val = (norm - 2.0 * dot_nt(cands, pts_ref[...])).reshape(FAR, ROUNDS, NZ, ROWS_DEV)
        least = jnp.min(jnp.min(val, axis=0), axis=1)
        for r in range(ROUNDS):
            rows_ref[pl.ds(r * NEAR + block, 1), :] = least[r : r + 1]


def own_kernel(base_ref, cands_ref, *refs):
    *pts_refs, rows_ref = refs
    rows_ref[ROUNDS * NEAR : ROUNDS * NEAR + 2, :] = base_ref[...]
    rows_ref[ROUNDS * NEAR + 2 :, :] = jnp.zeros((NEAR - 2, ROWS_DEV), F32)
    line_mins(cands_ref, pts_refs, rows_ref)


def other_kernel(own_ref, cands_ref, *refs):
    *pts_refs, out_ref, rows_ref = refs
    rows_ref[...] = own_ref[...]
    line_mins(cands_ref, pts_refs, rows_ref)
    rows = jnp.minimum(rows_ref[...], own_ref[...])
    for i in range(NEAR):
        out_ref[i] = rows


def last_kernel(recv_ref, run_ref, sums_ref, all_ref):
    def base_row(row):
        row += ROUNDS * NEAR
        return jnp.concatenate([recv_ref[(b - X_FIRST) % NEAR, row : row + 1] for b in range(NEAR)], axis=0)

    rows_norm = base_row(0)
    running = base_row(1)
    lane = iota((NZ * NC * NY, 128), 1)
    sums = jnp.where(lane == 0, jnp.sum(running), 0.0)
    for r in range(ROUNDS):
        least = recv_ref[0, r * NEAR : (r + 1) * NEAR]
        for s in range(1, NEAR):
            least = jnp.minimum(least, recv_ref[s, r * NEAR : (r + 1) * NEAR])
        running = jnp.minimum(running, jnp.maximum(rows_norm + least, 0.0))
        sums = jnp.where(lane == r + 1, jnp.sum(running), sums)
    for b in range(NEAR):
        all_ref[b] = running[b : b + 1]
    run_ref[...] = all_ref[lax.axis_index("x")]
    sums_ref[...] = sums


def final_kernel(recv_ref, run_ref, dist_ref, weight_ref, pot_ref):
    total = jnp.sum(recv_ref[...], axis=0, keepdims=True)
    lane = iota((1, 128), 1)
    last = jnp.sum(jnp.where(lane == ROUNDS, total, 0.0), axis=1, keepdims=True)
    running = run_ref[...]
    dist_ref[...] = running.reshape(ROWS_DEV)
    weight_ref[...] = (running * (ROWS / last)).reshape(ROWS_DEV)
    pot_ref[...] = total.reshape(128)[0 : ROUNDS + 1]


def vspec():
    return pl.BlockSpec(memory_space=VMEM)


def call(kernel, ins, outs, scratch=(), near=True):
    shapes = [VMEM(s, d) if near else jax.ShapeDtypeStruct(s, d) for s, d in outs]
    single = len(shapes) == 1
    kern = pl.pallas_call(
        kernel,
        in_specs=ins,
        out_specs=vspec() if single else [vspec() for _ in shapes],
        out_shape=shapes[0] if single else shapes,
        scratch_shapes=list(scratch),
        compiler_params=pltpu.CompilerParams(vmem_limit_bytes=16 << 20),
    )

    def run(*args):
        placed = []
        for a, i in zip(args, ins):
            space = VMEM if i.memory_space == VMEM else pltpu.HBM
            placed.append(pltpu.with_memory_space_constraint(a, space))
        return kern(*placed)

    return run


def body(points, first_center, counts, cand_index):
    pack = call(
        pack_kernel,
        [pl.BlockSpec(memory_space=pl.ANY)] * 3,
        [((PLANE, ROUNDS, CAP, D), BF16)],
        [
            SMEM((ROUNDS,), jnp.int32),
            SMEM((ROUNDS, 1, 1, CAP), jnp.int32),
            VMEM((ROWS_DEV, D), BF16),
            pltpu.SemaphoreType.DMA((3,)),
        ],
    )
    blocks = pack(counts.reshape(ROUNDS), cand_index, points)
    plane = ("y", "x")
    blocks, early = lax.optimization_barrier((blocks, points))
    blocks = lax.all_to_all(blocks, plane, 0, 0, axis_index_groups=PLANE_GROUP)
    compact = call(
        compact_kernel,
        [vspec()],
        [((NZ, ROUNDS * FOLD, LANES), BF16)],
        [VMEM((PLANE * SLOTS, D), F32), VMEM((ROUNDS * FOLD, LANES), F32)],
    )
    mine = compact(blocks)
    mine = lax.all_to_all(mine, "z", 0, 0, axis_index_groups=Z_GROUP)

    def from_side(rows, k):
        return lax.ppermute(rows, "x", [((i + k) % NX, i) for i in range(NX)])

    right = from_side(early, 1)
    far_side = lax.ppermute(right, "x", [((i + 1) % NX, i) for i in range(NX)])
    line = [points, right, far_side, from_side(early, 3)]
    base = call(base_kernel, [vspec()] * 2, [((2, ROWS_DEV), F32)])(points, first_center)
    spread = call(spread_kernel, [vspec()], [((FAR, KEEP, D), BF16)])
    mine = mine.reshape(NZ * ROUNDS * FOLD, LANES)
    cands = lax.all_to_all(spread(mine), "y", 0, 0, axis_index_groups=Y_GROUP).reshape(FAR * KEEP, D)
    others = lax.ppermute(cands, "c", [(0, 1), (1, 0)])
    rows = ((4 * NEAR, ROWS_DEV), F32)
    own = call(own_kernel, [vspec()] * (2 + NEAR), [rows])
    other = call(other_kernel, [vspec()] * (2 + NEAR), [((NEAR, *rows[0]), F32)], [VMEM(*rows)])
    mins = other(own(base, cands, *line), others, *line)
    mins = lax.all_to_all(mins, "x", 0, 0, axis_index_groups=X_GROUP)
    last = call(
        last_kernel,
        [vspec()],
        [((1, ROWS_DEV), F32), ((NZ * NC * NY, 128), F32)],
        [VMEM((NEAR, 1, ROWS_DEV), F32)],
    )
    running, sums = last(mins)
    sums = lax.all_to_all(sums, ("z", "c", "y"), 0, 0, axis_index_groups=SUM_GROUP)
    final = call(
        final_kernel,
        [vspec()] * 2,
        [((ROWS_DEV,), F32), ((ROWS_DEV,), F32), ((ROUNDS + 1,), F32)],
        near=False,
    )
    return tuple(final(sums, running))


def solution(mesh):
    axes = ("z", "c", "y", "x")
    grid = Mesh(mesh.devices.reshape(NZ, NC, NY, NX), axes)
    placed = (P(axes, None), P(), P(None, ("z", "c"), ("y", "x")), P(None, ("z", "c"), ("y", "x"), None))

    return jax.shard_map(
        body,
        mesh=grid,
        in_specs=placed,
        out_specs=(P(axes), P(axes), P()),
        check_vma=False,
    )
```
